256 devices in a mesh: seq: 8 (over y, core), chan: 32 (over z, x).
Axes of the slice: x: 4, y: 4, z: 8, core: 2. Of those that a mesh axis runs over, the one named last changes fastest.
Arguments:
- tokens: bfloat16 [1024, 4096], P('seq', 'chan'), may hold values from -6 to 6
- in_weight: bfloat16 [4096, 3, 4096], P(None, None, 'chan'), may hold values from -0.09375 to 0.09375
- short_kernel: float32 [3, 3, 4096], P(None, None, 'chan'), may hold values from -3 to 3
- filters: float32 [2, 1024, 4096], P(None, 'seq', 'chan'), may hold values from -0.5 to 0.5
- skip_gain: float32 [2, 4096], P(None, 'chan'), may hold values from 0.5 to 1.5
- out_weight: bfloat16 [4096, 4096], P('chan'), may hold values from -0.09375 to 0.09375
- cotangent: bfloat16 [1024, 4096], P('seq', 'chan'), may hold values from -6 to 6
Outputs:
- mixed: bfloat16 [1024, 4096], P('seq', 'chan')
- token_grad: bfloat16 [1024, 4096], P('seq', 'chan')
The draws below stay inside these ranges and needn't reach their ends.
All inputs are finite; a program needn't handle non-finite values.
Results may differ from the reference program's by a relative error of at most 0.0049.
Values may be sent and summed in bfloat16 or wider, within the bound.
No kernel may reach another device: no remote copies, remote signals or barrier semaphores. Data moves between devices by JAX's collectives and lax.ppermute only.
A program may use at most 64 MiB of HBM per device.

```python
import math
import jax
import jax.numpy as jnp
from jax import lax

D = 4096
SHORT = 3
SEQUENCE_LENGTH = 1024


def draw_filters(key, part):
    base_key = jax.random.fold_in(key, 7)
    random_key_sequence = jax.random.split(base_key, 5)
    slow_share = 0.5
    noise_part = jnp.clip(jax.random.normal(random_key_sequence[0], (2, SEQUENCE_LENGTH, D), jnp.float32), -4.0, 4.0)
    chooser = jax.random.uniform(random_key_sequence[1], (2, 1, D), jnp.float32)
    fast_len = jnp.exp(jax.random.uniform(random_key_sequence[2], (2, 1, D), jnp.float32, math.log(30.0), math.log(50.0)))
    slow_len = SEQUENCE_LENGTH * jnp.exp(jax.random.uniform(random_key_sequence[3], (2, 1, D), jnp.float32, 0.0, math.log(4.0)))
    reach = jnp.where(chooser < slow_share, slow_len, fast_len)
    transfer_rounds = jax.random.randint(random_key_sequence[4], (2, 1, 1, 2), 1, SEQUENCE_LENGTH)
    token_positions = jnp.arange(SEQUENCE_LENGTH, dtype=jnp.int32)[None, :, None, None]
    received_piece = jnp.sum((token_positions >= transfer_rounds).astype(jnp.float32), axis=-1)
    steps_float = jnp.arange(SEQUENCE_LENGTH, dtype=jnp.float32)[None, :, None]
    envelope = jnp.exp(-steps_float / reach) * jnp.power(0.6, received_piece)
    return jnp.clip(noise_part * envelope * jax.lax.rsqrt(reach), -0.5, 0.5)


def steps_of(key, shape, cuts, smallest, high):
    gain, own = 1.0, jax.random.fold_in(key, 6)
    for axis_at, shards_of in cuts:
        draws = jnp.exp(jax.random.uniform(jax.random.fold_in(own, axis_at), (shards_of,), jnp.float32, smallest / len(cuts), high / len(cuts)))
        gain = gain * jnp.repeat(draws, shape[axis_at] // shards_of).reshape([-1 if axis == axis_at else 1 for axis in range(len(shape))])
    return gain


def bell_draw(rng, dims, spread, most, cuts=(), held_as=jnp.bfloat16):
    result = spread * jax.random.normal(rng, dims, jnp.float32)
    if cuts:
        result = result * steps_of(rng, dims, cuts, -0.22, 0.18)
    return jnp.clip(result, -most, most).astype(held_as)


def setup_inputs(seed: int = 0) -> dict:
    arg_keys = jax.random.split(jax.random.key(seed), 8)
    return {
        "tokens": bell_draw(arg_keys[0], (SEQUENCE_LENGTH, D), 1.0, 6.0, ((0, 8), (1, 32))),
        "in_weight": bell_draw(arg_keys[1], (D, 3, D), D ** -0.5, 0.09375, ((2, 32),)),
        "short_kernel": bell_draw(arg_keys[2], (SHORT, 3, D), 0.6, 3.0, ((2, 32),), jnp.float32),
        "filters": draw_filters(jax.random.fold_in(arg_keys[7], 71), 0),
        "skip_gain": jnp.clip(0.5 + 1.0 * jax.random.uniform(arg_keys[4], (2, D), jnp.float32) ** steps_of(arg_keys[4], (2, D), ((1, 32),), -0.2, 0.2), 0.5, 1.5),
        "out_weight": bell_draw(arg_keys[5], (D, D), D ** -0.5, 0.09375, ((0, 32),)),
        "cotangent": bell_draw(arg_keys[6], (SEQUENCE_LENGTH, D), 1.0, 6.0, ((0, 8), (1, 32))),
    }


def lag_rows(array, shift_by):
    return jnp.pad(array, ((shift_by, 0), (0, 0), (0, 0)))[:array.shape[0]]


def lead_rows(array, shift_by):
    return jnp.pad(array, ((0, shift_by), (0, 0), (0, 0)))[shift_by:]


def causal_conv(signal, filter_rows, conjugate):
    n_total = 2 * SEQUENCE_LENGTH
    signal_spec = jnp.fft.rfft(signal, n=n_total, axis=0)
    filter_spec = jnp.fft.rfft(filter_rows, n=n_total, axis=0)
    if conjugate:
        filter_spec = jnp.conj(filter_spec)
    return jnp.fft.irfft(signal_spec * filter_spec, n=n_total, axis=0)[:SEQUENCE_LENGTH].astype(jnp.float32)


def reference(tokens, in_weight, short_kernel, filters, skip_gain, out_weight, cotangent):
    width = in_weight.shape[0]
    flat_in = in_weight.reshape((width, 3 * width))
    projected = jnp.dot(tokens, flat_in, preferred_element_type=jnp.float32).reshape((SEQUENCE_LENGTH, 3, width))
    shorted = short_kernel[0] * projected
    for tap_index in range(1, SHORT):
        shorted = shorted + short_kernel[tap_index] * lag_rows(projected, tap_index)
    values = shorted[:, 0]
    gate_one = shorted[:, 1]
    gate_two = shorted[:, 2]
    conv_one = causal_conv(values, filters[0], False) + skip_gain[0] * values
    first_out = gate_one * conv_one
    conv_two = causal_conv(first_out, filters[1], False) + skip_gain[1] * first_out
    second_order_output = (gate_two * conv_two).astype(jnp.bfloat16)
    mixed = jnp.dot(second_order_output, out_weight, preferred_element_type=jnp.float32).astype(jnp.bfloat16)
    grad_two = lax.dot_general(cotangent, out_weight, (((1,), (1,)), ((), ())), preferred_element_type=jnp.float32)
    grad_gate_two = grad_two * conv_two
    grad_conv_two = grad_two * gate_two
    grad_first = causal_conv(grad_conv_two, filters[1], True) + skip_gain[1] * grad_conv_two
    first_gate_gradient = grad_first * conv_one
    grad_conv_one = grad_first * gate_one
    grad_values = causal_conv(grad_conv_one, filters[0], True) + skip_gain[0] * grad_conv_one
    grad_short = jnp.stack([grad_values, first_gate_gradient, grad_gate_two], axis=1)
    grad_proj = short_kernel[0] * grad_short
    for tap_index in range(1, SHORT):
        grad_proj = grad_proj + short_kernel[tap_index] * lead_rows(grad_short, tap_index)
    grad_flat = grad_proj.reshape((SEQUENCE_LENGTH, 3 * width)).astype(jnp.bfloat16)
    token_grad = lax.dot_general(grad_flat, flat_in, (((1,), (1,)), ((), ())), preferred_element_type=jnp.float32)
    return mixed, token_grad.astype(jnp.bfloat16)
```

```python
import functools
import math

import jax
import jax.numpy as jnp
import numpy as np
from jax import lax
from jax.experimental import pallas as pl
from jax.experimental.pallas import tpu as pltpu
from jax.sharding import Mesh, PartitionSpec as P


F32 = jnp.float32
BF16 = jnp.bfloat16
LANES = 128
BLOCKS = 8
COARSE = 2 * BLOCKS
KEPT = COARSE // 2 + 1
SEQ = ("y", "core")


def fine_table():
    ids = np.arange(LANES)
    angle = 2.0 * np.pi / LANES * (ids[:, None] * ids[None, :] % LANES)
    table = np.stack([np.cos(angle), np.sin(angle)]).astype(np.float32)
    high = table.astype(jnp.bfloat16)
    low = (table - high.astype(np.float32)).astype(jnp.bfloat16)
    return np.stack([high, low])


def fine_matrices(table_ref):
    found = []
    for part in range(2):
        cosine, sine = table_ref[part, 0], table_ref[part, 1]
        upper = jnp.concatenate([cosine, -sine], axis=1)
        found.append(jnp.concatenate([upper, jnp.concatenate([sine, cosine], axis=1)], axis=0))
    return found


def twiddle_table():
    angle = (
        2.0 * np.pi / (COARSE * LANES) * (np.arange(KEPT)[:, None] * np.arange(LANES)[None, :])
    )
    return np.stack([np.cos(angle), np.sin(angle)]).astype(np.float32)


def coarse(index):
    index = index % COARSE
    cosine = math.cos(2.0 * math.pi * index / COARSE)
    sine = math.sin(2.0 * math.pi * index / COARSE)
    return cosine, sine


def add_term(total, value, factor):
    if abs(factor) < 1e-9:
        return total
    if abs(abs(factor) - 1.0) < 1e-9:
        if total is None:
            return value if factor > 0 else -value
        return total + value if factor > 0 else total - value
    return value * factor if total is None else total + value * factor


def precise_dot(value, matrices):
    high = value.astype(BF16)
    low = (value - high.astype(F32)).astype(BF16)
    dot = functools.partial(jnp.dot, preferred_element_type=F32)
    return (dot(low, matrices[0]) + dot(high, matrices[1])) + dot(high, matrices[0])


def spectrum(signal, matrices, twiddle_ref):
    parts = []
    for freq in range(KEPT):
        real = imag = None
        for block in range(BLOCKS):
            cosine, sine = coarse(block * freq)
            real = add_term(real, signal[block], cosine)
            imag = add_term(imag, signal[block], -sine)
        cos_t = twiddle_ref[0, freq : freq + 1, :]
        sin_t = twiddle_ref[1, freq : freq + 1, :]
        if imag is None:
            turned = (real * cos_t, -real * sin_t)
        else:
            turned = (real * cos_t + imag * sin_t, imag * cos_t - real * sin_t)
        parts.append(jnp.concatenate(turned, axis=1))
    return precise_dot(jnp.concatenate(parts, axis=0), matrices)


def restore(turned_spec, matrices, twiddle_ref):
    rows = turned_spec.shape[0] // KEPT
    back = precise_dot(turned_spec, matrices)
    real, imag = [], []
    for freq in range(KEPT):
        piece = back[freq * rows : (freq + 1) * rows]
        re, minus_im = piece[:, :LANES], piece[:, LANES:]
        cos_t = twiddle_ref[0, freq : freq + 1, :]
        sin_t = twiddle_ref[1, freq : freq + 1, :]
        real.append(re * cos_t + minus_im * sin_t)
        imag.append(re * sin_t - minus_im * cos_t)
    out = []
    for block in range(BLOCKS):
        total = None
        for freq in range(1, KEPT - 1):
            cosine, sine = coarse(block * freq)
            total = add_term(total, real[freq], cosine)
            total = add_term(total, imag[freq], -sine)
        total = 2.0 * total + real[0]
        out.append(add_term(total, real[KEPT - 1], 1.0 if block % 2 == 0 else -1.0))
    return out


def turned_product(left, right, conjugate):
    left_re, left_im = left[:, :LANES], left[:, LANES:]
    right_re, right_im = right[:, :LANES], right[:, LANES:]
    straight, crossed = left_re * right_re, left_im * right_im
    if conjugate:
        real, minus_imag = straight + crossed, left_re * right_im - left_im * right_re
    else:
        real, minus_imag = straight - crossed, -(left_re * right_im + left_im * right_re)
    return jnp.concatenate([real, minus_imag], axis=1)


def lagged(blocks, steps):
    lane = lax.broadcasted_iota(jnp.int32, blocks[0].shape, 1)
    turned = [pltpu.roll(block, steps, 1) for block in blocks]
    before = [jnp.zeros_like(blocks[0])] + turned[:-1]
    return [jnp.where(lane >= steps, own, prior) for own, prior in zip(turned, before)]


def leading(blocks, steps):
    lane = lax.broadcasted_iota(jnp.int32, blocks[0].shape, 1)
    turned = [pltpu.roll(block, LANES - steps, 1) for block in blocks]
    after = turned[1:] + [jnp.zeros_like(blocks[0])]
    return [jnp.where(lane < LANES - steps, own, later) for own, later in zip(turned, after)]


def short_sum(blocks, coef_ref, which, shift):
    total = [coef_ref[which] * block for block in blocks]
    for tap in (1, 2):
        factor = coef_ref[3 * tap + which]
        total = [have + factor * block for have, block in zip(total, shift(blocks, tap))]
    return total


def operator_kernel(
    table_hbm, twiddle_hbm, given_ref, coef_ref, out_ref, table_ref, twiddle_ref, sems
):
    count = given_ref.shape[1] // 6
    tables_in = [
        *started([table_hbm], [table_ref], sems.at[0]),
        *started([twiddle_hbm], [twiddle_ref], sems.at[1]),
    ]

    def rows_of(slot):
        return [given_ref[block, slot * count : (slot + 1) * count] for block in range(BLOCKS)]

    def store(slot, blocks):
        for block, value in enumerate(blocks):
            out_ref[block, slot * count : (slot + 1) * count] = value.astype(BF16)

    def scaled(gain, blocks):
        return [coef_ref[gain] * value for value in blocks]

    def product(left, right):
        return [one * two for one, two in zip(left, right)]

    def plus(left, right):
        return [one + two for one, two in zip(left, right)]

    def filtered(blocks, order, conjugate):
        spec = turned_product(
            spectrum(blocks, matrices, twiddle_ref), filter_spec[order], conjugate
        )
        return plus(restore(spec, matrices, twiddle_ref), scaled(9 + order, blocks))

    values = short_sum(rows_of(0), coef_ref, 0, lagged)
    gate_one = short_sum(rows_of(1), coef_ref, 1, lagged)
    gate_two = short_sum(rows_of(2), coef_ref, 2, lagged)
    for copy in tables_in:
        copy.wait()
    matrices = fine_matrices(table_ref)
    filter_spec = [
        spectrum(rows_of(3 + order), matrices, twiddle_ref) * (1.0 / (COARSE * LANES))
        for order in range(2)
    ]
    conv_one = filtered(values, 0, False)
    conv_two = filtered(product(gate_one, conv_one), 1, False)
    store(0, product(gate_two, conv_two))
    grad_two = rows_of(5)
    store(3, short_sum(product(grad_two, conv_two), coef_ref, 2, leading))
    grad_first = filtered(product(grad_two, gate_two), 1, True)
    store(2, short_sum(product(grad_first, conv_one), coef_ref, 1, leading))
    grad_values = filtered(product(grad_first, gate_one), 0, True)
    store(1, short_sum(grad_values, coef_ref, 0, leading))


def started(source_refs, targets, sems):
    found = []
    for at, (source, target) in enumerate(zip(source_refs, targets)):
        copy = pltpu.make_async_copy(source, target, sems.at[at])
        copy.start()
        found.append(copy)
    return found


def weight_start(place_ref, z, apart, ring, feats):
    block = z * ring + lax.rem(place_ref[0] + apart, ring)
    return pl.multiple_of(block * feats, feats)


def chunks(ref, parts, axis):
    size = ref.shape[axis] // parts
    lead = (slice(None),) * axis
    return [ref.at[(*lead, pl.ds(part * size, size))] for part in range(parts)]


def project_kernel(
    ring,
    place_ref,
    weight_ref,
    filter_ref,
    own,
    left,
    right,
    far,
    out_ref,
    held,
    held_filter,
    sems,
):
    n_z, tokens, feats = own.shape
    (filter_copy,) = started([filter_ref], [held_filter], sems.at[1])
    copies_in = started(chunks(weight_ref, n_z, 1), chunks(held, n_z, 1), sems.at[0])
    chans = weight_ref.shape[2]
    count = chans // BLOCKS

    def store(slot, turned):
        for block in range(BLOCKS):
            out_ref[block, slot * count : (slot + 1) * count] = turned[
                block * count : (block + 1) * count
            ]

    filter_copy.wait()
    for order in range(2):
        store(3 + order, held_filter[order].T)
    total = [jnp.zeros((tokens, chans), F32)] * 3
    for z in range(n_z):
        copies_in[z].wait()
        for rows_ref, apart in ((own, 0), (right, 1), (far, 2), (left, 3)):
            start = weight_start(place_ref, z, apart, ring, feats)
            for which in range(3):
                total[which] = total[which] + jnp.dot(
                    rows_ref[z], held[which, pl.ds(start, feats), :], preferred_element_type=F32
                )
    for which in range(3):
        store(which, total[which].T)


def project_grad_kernel(
    ring, place_ref, weight_ref, own, left, right, far, given_ref, out_ref, held, sems
):
    n_z, tokens, feats = own.shape
    copies_in = started(chunks(weight_ref, n_z, 1), chunks(held, n_z, 1), sems)
    total = jnp.zeros((weight_ref.shape[0], tokens), F32)
    for z in range(n_z):
        copies_in[z].wait()
        for rows_ref, apart in ((own, 0), (right, 1), (far, 2), (left, 3)):
            start = weight_start(place_ref, z, apart, ring, feats)
            total = total + lax.dot_general(
                held[:, pl.ds(start, feats)],
                rows_ref[z],
                (((1,), (1,)), ((), ())),
                preferred_element_type=F32,
            )
    count = out_ref.shape[1] // 6
    out_ref[:, : 5 * count] = given_ref[...]
    out_ref[:, 5 * count :] = total.reshape((BLOCKS, count, tokens))


def partial_kernel(
    ring,
    place_ref,
    out_weight_ref,
    in_weight_ref,
    channels_ref,
    own_ref,
    right_ref,
    left_ref,
    keep_r_ref,
    keep_l_ref,
    held_out,
    held_in,
    sems,
):
    n_z, _, feats, tokens = own_ref.shape
    half = n_z // 2
    out_copies = started(chunks(out_weight_ref, n_z, 1), chunks(held_out, n_z, 1), sems.at[0])
    in_copies = started(chunks(in_weight_ref, n_z, 1), chunks(held_in, n_z, 1), sems.at[1])
    count = channels_ref.shape[1] // 4
    second, *grads = [
        channels_ref[:, slot * count : (slot + 1) * count].reshape((BLOCKS * count, tokens))
        for slot in range(4)
    ]
    second = second.astype(F32).T.astype(BF16)
    dot = functools.partial(jnp.dot, preferred_element_type=F32)

    def mixed(z, apart):
        start = weight_start(place_ref, z, apart, ring, feats)
        return dot(second, held_out[:, pl.ds(start, feats)])

    def token_grad(z, apart):
        start = weight_start(place_ref, z, apart, ring, feats)
        total = dot(held_in[0, pl.ds(start, feats), :], grads[0])
        for which in (1, 2):
            total = total + dot(held_in[which, pl.ds(start, feats), :], grads[which])
        return total

    for copy in out_copies + in_copies:
        copy.wait()
    for output, product in ((0, mixed), (1, token_grad)):
        for z in range(n_z):
            own_ref[z, output] = product(z, 0).astype(BF16)
            if z < half:
                right_ref[z, output] = product(z, 2).astype(BF16)
                keep_r_ref[z, output] = product(z, 1).astype(BF16)
                left_ref[z, output] = product(z, 3).astype(BF16)
            else:
                right_ref[z, output] = product(z, 1).astype(BF16)
                left_ref[z, output] = product(z, 2).astype(BF16)
                keep_l_ref[z - half, output] = product(z, 3).astype(BF16)


def merge_kernel(keep_r_ref, keep_l_ref, from_l_ref, from_r_ref, right_ref, left_ref):
    half = keep_r_ref.shape[0]
    right_ref[...] = (keep_r_ref[...].astype(F32) + from_l_ref[:half].astype(F32)).astype(BF16)
    left_ref[...] = (keep_l_ref[...].astype(F32) + from_r_ref[half:].astype(F32)).astype(BF16)


def ring_sum_kernel(own_ref, from_l_ref, from_r_ref, last_l_ref, last_r_ref, out_ref):
    half = last_l_ref.shape[0]
    own_low, own_high = own_ref[:half].astype(F32), own_ref[half:].astype(F32)
    out_ref[:half] = (
        own_low + last_l_ref[...].astype(F32) + from_r_ref[:half].astype(F32)
    ).astype(BF16)
    out_ref[half:] = (
        own_high + from_l_ref[half:].astype(F32) + last_r_ref[...].astype(F32)
    ).astype(BF16)


def last_sum_kernel(parts_ref, mixed_ref, token_grad_ref):
    totals = []
    for output in range(2):
        total = parts_ref[0, output].astype(F32)
        for part in range(1, parts_ref.shape[0]):
            total = total + parts_ref[part, output].astype(F32)
        totals.append(total)
    mixed_ref[...] = totals[0].astype(BF16)
    token_grad_ref[...] = totals[1].T.astype(BF16)


def run(kernel, out_shape, *args, flops=0, place=None, weights=()):
    single = not isinstance(out_shape, (list, tuple))
    outs = (out_shape,) if single else out_shape
    in_vmem = pl.BlockSpec(memory_space=pltpu.VMEM)
    specs, scratch = [in_vmem] * len(args), []
    if weights:
        held = (pltpu.with_memory_space_constraint(weight, pltpu.HBM) for weight in weights)
        places = () if place is None else (place,)
        args = (*places, *held, *args)
        in_hbm = [pl.BlockSpec(memory_space=pltpu.HBM)] * len(weights)
        specs = [pl.BlockSpec(memory_space=pltpu.SMEM)] * len(places) + in_hbm + specs
        scratch = [pltpu.VMEM(weight.shape, weight.dtype) for weight in weights]
        shape = (BLOCKS,) if len(weights) == 1 else (len(weights), BLOCKS)
        scratch.append(pltpu.SemaphoreType.DMA(shape))
    moved = sum(int(np.prod(a.shape)) * a.dtype.itemsize for a in (*args, *outs))
    return pl.pallas_call(
        kernel,
        out_shape=out_shape,
        in_specs=specs,
        out_specs=in_vmem if single else [in_vmem] * len(outs),
        scratch_shapes=scratch,
        compiler_params=pltpu.CompilerParams(vmem_limit_bytes=24 << 20),
        cost_estimate=pl.CostEstimate(flops=flops, bytes_accessed=moved, transcendentals=0),
    )(*args)


def shape_of(shape, dtype):
    return jax.ShapeDtypeStruct(shape, dtype)


def exchanged(value, axis):
    return lax.all_to_all(value, axis, 0, 0, tiled=True)


def copies(value, count):
    return jnp.broadcast_to(value[None], (count, *value.shape))


def shifted(value, steps):
    ring = lax.axis_size("x")
    return lax.ppermute(value, "x", [(at, (at + steps) % ring) for at in range(ring)])


def after(value, *others):
    return lax.optimization_barrier((value, *others))[0]


def gathered(own, steps):
    left, right = shifted(own, 1), shifted(own, -1)
    return left, right, shifted(left if steps > 0 else right, steps)


def on_device(tokens, in_weight, short_kernel, filters, skip_gain, out_weight, cotangent):
    width, _, chans = in_weight.shape
    rows = tokens.shape[0]
    n_z, ring = lax.axis_size("z"), lax.axis_size("x")
    half = n_z // 2
    count = chans // BLOCKS
    seq_index = lax.axis_index(SEQ)
    place = lax.axis_index("x").reshape((1,)).astype(jnp.int32)
    table = jnp.asarray(fine_table())
    twiddles = jnp.asarray(twiddle_table())
    split_in = in_weight.transpose((1, 0, 2))

    taps = lax.dynamic_slice_in_dim(short_kernel, seq_index * count, count, 2)
    gains = lax.dynamic_slice_in_dim(skip_gain, seq_index * count, count, 1)
    coef = jnp.concatenate([taps.reshape((9, count)), gains], axis=0)
    coef = jnp.broadcast_to(coef[:, :, None], (11, count, LANES))

    own_rows = exchanged(copies(tokens, n_z), "z")
    own_grads = exchanged(after(copies(cotangent, n_z), own_rows), "z")
    other_rows = gathered(own_rows, 1)
    other_grads = gathered(after(own_grads, *other_rows[:2]), -1)

    given = run(
        functools.partial(project_kernel, ring),
        shape_of((BLOCKS, 5 * count, rows), F32),
        own_rows,
        *other_rows,
        flops=2 * rows * width * 3 * chans,
        place=place,
        weights=(split_in, filters),
    )
    given = run(
        functools.partial(project_grad_kernel, ring),
        shape_of((BLOCKS, 6 * count, rows), F32),
        own_grads,
        *other_grads,
        given,
        flops=2 * rows * width * chans,
        place=place,
        weights=(out_weight,),
    )
    channels = run(
        operator_kernel,
        shape_of((BLOCKS, 4 * count, LANES), BF16),
        exchanged(given, SEQ),
        coef,
        weights=(table, twiddles),
    )
    whole, part = (n_z, 2, LANES, rows), (half, 2, LANES, rows)
    own, to_right, to_left, keep_r, keep_l = run(
        functools.partial(partial_kernel, ring),
        tuple(shape_of(shape, BF16) for shape in (whole, whole, whole, part, part)),
        exchanged(channels, SEQ),
        flops=2 * rows * width * 4 * chans,
        place=place,
        weights=(out_weight, split_in),
    )
    from_l, from_r = shifted(to_right, 1), shifted(to_left, -1)
    to_right, to_left = run(
        merge_kernel, (shape_of(part, BF16), shape_of(part, BF16)), keep_r, keep_l, from_l, from_r
    )
    last_l, last_r = shifted(to_right, 1), shifted(to_left, -1)
    parts = run(ring_sum_kernel, shape_of(whole, BF16), own, from_l, from_r, last_l, last_r)
    out = shape_of((rows, LANES), BF16)
    return run(last_sum_kernel, (out, out), exchanged(parts, "z"))


def solution(mesh):
    split = Mesh(mesh.devices.reshape((4, 2, 8, 4)), ("y", "core", "z", "x"))
    chan = ("z", "x")
    in_specs = (
        P(SEQ, chan),
        P(None, None, chan),
        P(None, None, chan),
        P(None, SEQ, chan),
        P(None, chan),
        P(chan, None),
        P(SEQ, chan),
    )
    out_specs = (P(SEQ, chan), P(SEQ, chan))

    return jax.shard_map(
        on_device, mesh=split, in_specs=in_specs, out_specs=out_specs, check_vma=False
    )
```

```python
import functools
import math

import jax
import jax.numpy as jnp
import numpy as np
from jax import lax
from jax.experimental import pallas as pl
from jax.experimental.pallas import tpu as pltpu
from jax.sharding import Mesh, PartitionSpec as P


F32 = jnp.float32
BF16 = jnp.bfloat16
LANES = 128
BLOCKS = 8
COARSE = 2 * BLOCKS
KEPT = COARSE // 2 + 1
SEQ = ("y", "core")


def fine_table():
    ids = np.arange(LANES)
    angle = 2.0 * np.pi / LANES * (ids[:, None] * ids[None, :] % LANES)
    table = np.stack([np.cos(angle), np.sin(angle)]).astype(np.float32)
    high = table.astype(jnp.bfloat16)
    low = (table - high.astype(np.float32)).astype(jnp.bfloat16)
    return np.stack([high, low])


def fine_matrices(table_ref):
    found = []
    for part in range(2):
        cosine, sine = table_ref[part, 0], table_ref[part, 1]
        upper = jnp.concatenate([cosine, -sine], axis=1)
        found.append(jnp.concatenate([upper, jnp.concatenate([sine, cosine], axis=1)], axis=0))
    return found


def twiddle_table():
    angle = (
        2.0 * np.pi / (COARSE * LANES) * (np.arange(KEPT)[:, None] * np.arange(LANES)[None, :])
    )
    return np.stack([np.cos(angle), np.sin(angle)]).astype(np.float32)


def coarse(index):
    index = index % COARSE
    cosine = math.cos(2.0 * math.pi * index / COARSE)
    sine = math.sin(2.0 * math.pi * index / COARSE)
    return cosine, sine


def add_term(total, value, factor):
    if abs(factor) < 1e-9:
        return total
    if abs(abs(factor) - 1.0) < 1e-9:
        if total is None:
            return value if factor > 0 else -value
        return total + value if factor > 0 else total - value
    return value * factor if total is None else total + value * factor


def precise_dot(value, matrices):
    high = value.astype(BF16)
    low = (value - high.astype(F32)).astype(BF16)
    dot = functools.partial(jnp.dot, preferred_element_type=F32)
    return (dot(low, matrices[0]) + dot(high, matrices[1])) + dot(high, matrices[0])


def spectrum(signal, matrices, twiddle_ref):
    parts = []
    for freq in range(KEPT):
        real = imag = None
        for block in range(BLOCKS):
            cosine, sine = coarse(block * freq)
            real = add_term(real, signal[block], cosine)
            imag = add_term(imag, signal[block], -sine)
        cos_t = twiddle_ref[0, freq : freq + 1, :]
        sin_t = twiddle_ref[1, freq : freq + 1, :]
        if imag is None:
            turned = (real * cos_t, -real * sin_t)
        else:
            turned = (real * cos_t + imag * sin_t, imag * cos_t - real * sin_t)
        parts.append(jnp.concatenate(turned, axis=1))
    return precise_dot(jnp.concatenate(parts, axis=0), matrices)


def restore(turned_spec, matrices, twiddle_ref):
    rows = turned_spec.shape[0] // KEPT
    back = precise_dot(turned_spec, matrices)
    real, imag = [], []
    for freq in range(KEPT):
        piece = back[freq * rows : (freq + 1) * rows]
        re, minus_im = piece[:, :LANES], piece[:, LANES:]
        cos_t = twiddle_ref[0, freq : freq + 1, :]
        sin_t = twiddle_ref[1, freq : freq + 1, :]
        real.append(re * cos_t + minus_im * sin_t)
        imag.append(re * sin_t - minus_im * cos_t)
    out = []
    for block in range(BLOCKS):
        total = None
        for freq in range(1, KEPT - 1):
            cosine, sine = coarse(block * freq)
            total = add_term(total, real[freq], cosine)
            total = add_term(total, imag[freq], -sine)
        total = 2.0 * total + real[0]
        out.append(add_term(total, real[KEPT - 1], 1.0 if block % 2 == 0 else -1.0))
    return out


def turned_product(left, right, conjugate):
    left_re, left_im = left[:, :LANES], left[:, LANES:]
    right_re, right_im = right[:, :LANES], right[:, LANES:]
    straight, crossed = left_re * right_re, left_im * right_im
    if conjugate:
        real, minus_imag = straight + crossed, left_re * right_im - left_im * right_re
    else:
        real, minus_imag = straight - crossed, -(left_re * right_im + left_im * right_re)
    return jnp.concatenate([real, minus_imag], axis=1)


def lagged(blocks, steps):
    lane = lax.broadcasted_iota(jnp.int32, blocks[0].shape, 1)
    turned = [pltpu.roll(block, steps, 1) for block in blocks]
    before = [jnp.zeros_like(blocks[0])] + turned[:-1]
    return [jnp.where(lane >= steps, own, prior) for own, prior in zip(turned, before)]


def leading(blocks, steps):
    lane = lax.broadcasted_iota(jnp.int32, blocks[0].shape, 1)
    turned = [pltpu.roll(block, LANES - steps, 1) for block in blocks]
    after = turned[1:] + [jnp.zeros_like(blocks[0])]
    return [jnp.where(lane < LANES - steps, own, later) for own, later in zip(turned, after)]


def short_sum(blocks, coef_ref, which, shift):
    total = [coef_ref[which] * block for block in blocks]
    for tap in (1, 2):
        factor = coef_ref[3 * tap + which]
        total = [have + factor * block for have, block in zip(total, shift(blocks, tap))]
    return total


def operator_kernel(
    place_ref,
    table_hbm,
    twiddle_hbm,
    taps_hbm,
    gains_hbm,
    given_ref,
    filter_ref,
    out_ref,
    table_ref,
    twiddle_ref,
    taps_ref,
    gains_ref,
    rows_ref,
    turned_ref,
    coef_ref,
    sems,
):
    count = given_ref.shape[1] // 4
    tables_in = [
        *started([table_hbm], [table_ref], sems.at[0]),
        *started([twiddle_hbm], [twiddle_ref], sems.at[1]),
    ]
    coef_in = [
        *started([taps_hbm], [taps_ref], sems.at[2]),
        *started([gains_hbm], [gains_ref], sems.at[3]),
    ]
    for copy in coef_in:
        copy.wait()
    rows_ref[...] = jnp.zeros_like(rows_ref)
    for tap in range(3):
        for which in range(3):
            rows_ref[3 * tap + which] = taps_ref[tap, which]
    for order in range(2):
        rows_ref[9 + order] = gains_ref[order]
    turned_ref[...] = rows_ref[...].T
    own_start = pl.multiple_of(place_ref[0] * count, count)
    columns = turned_ref[pl.ds(own_start, count), :]
    for at in range(coef_ref.shape[0]):
        coef_ref[at] = jnp.broadcast_to(columns[:, at : at + 1], coef_ref.shape[1:])

    def rows_of(slot, ref=given_ref):
        return [ref[block, slot * count : (slot + 1) * count] for block in range(BLOCKS)]

    def store(slot, blocks):
        for block, value in enumerate(blocks):
            out_ref[block, slot * count : (slot + 1) * count] = value.astype(BF16)

    def scaled(gain, blocks):
        return [coef_ref[gain] * value for value in blocks]

    def product(left, right):
        return [one * two for one, two in zip(left, right)]

    def plus(left, right):
        return [one + two for one, two in zip(left, right)]

    def filtered(blocks, order, conjugate):
        spec = turned_product(
            spectrum(blocks, matrices, twiddle_ref), filter_spec[order], conjugate
        )
        return plus(restore(spec, matrices, twiddle_ref), scaled(9 + order, blocks))

    values = short_sum(rows_of(0), coef_ref, 0, lagged)
    gate_one = short_sum(rows_of(1), coef_ref, 1, lagged)
    gate_two = short_sum(rows_of(2), coef_ref, 2, lagged)
    for copy in tables_in:
        copy.wait()
    matrices = fine_matrices(table_ref)
    filter_spec = [
        spectrum(rows_of(order, filter_ref), matrices, twiddle_ref) * (1.0 / (COARSE * LANES))
        for order in range(2)
    ]
    conv_one = filtered(values, 0, False)
    conv_two = filtered(product(gate_one, conv_one), 1, False)
    store(0, product(gate_two, conv_two))
    grad_two = rows_of(3)
    store(3, short_sum(product(grad_two, conv_two), coef_ref, 2, leading))
    grad_first = filtered(product(grad_two, gate_two), 1, True)
    store(2, short_sum(product(grad_first, conv_one), coef_ref, 1, leading))
    grad_values = filtered(product(grad_first, gate_one), 0, True)
    store(1, short_sum(grad_values, coef_ref, 0, leading))


def started(source_refs, targets, sems):
    found = []
    for at, (source, target) in enumerate(zip(source_refs, targets)):
        copy = pltpu.make_async_copy(source, target, sems.at[at])
        copy.start()
        found.append(copy)
    return found


def copies_kernel(tokens_hbm, cotangent_hbm, out_ref, held, sems):
    begun = started([tokens_hbm, cotangent_hbm], [held.at[0], held.at[1]], sems)
    for copy in begun:
        copy.wait()
    for at in range(out_ref.shape[0]):
        out_ref[at] = held[...]


def apart_kernel(both_ref, rows_ref, grads_ref):
    rows_ref[...] = both_ref[:, 0]
    grads_ref[...] = both_ref[:, 1]


def turned_filters_kernel(filter_ref, out_ref):
    count = out_ref.shape[1] // 2
    for order in range(2):
        turned = filter_ref[order].T
        for block in range(BLOCKS):
            out_ref[block, order * count : (order + 1) * count] = turned[
                block * count : (block + 1) * count
            ]


def out_weight_copies(place_ref, out_hbm, out_ref, sems):
    ring, n_z = sems.shape
    feats = out_ref.shape[1] // (ring * n_z)
    begun = []
    for z in range(n_z):
        for apart in range(ring):
            source = lax.rem(place_ref[0] + apart, ring)
            start = pl.multiple_of((z * ring + source) * feats, feats)
            copy = pltpu.make_async_copy(
                out_hbm.at[:, pl.ds(start, feats)],
                out_ref.at[:, pl.ds((z * ring + apart) * feats, feats)],
                sems.at[apart, z],
            )
            copy.start()
            begun.append(copy)
    return begun


def weights_kernel(place_ref, in_hbm, out_hbm, in_ref, out_ref, in_sems, out_sems):
    parts, _, ring, _, chans = in_hbm.shape
    begun = []
    for apart in range(ring):
        source = lax.rem(place_ref[0] + apart, ring)
        for part in range(parts):
            copy = pltpu.make_async_copy(
                in_hbm.at[part, :, source],
                in_ref.at[:, apart, :, pl.ds(part * chans, chans)],
                in_sems.at[apart, part],
            )
            copy.start()
            begun.append(copy)
    begun += out_weight_copies(place_ref, out_hbm, out_ref, out_sems)
    for copy in begun:
        copy.wait()


def side_by_side(own, right, far, left, z):
    return jnp.concatenate([own[z], right[z], far, left[z]], axis=1)


def project_kernel(weight_ref, own, left, right, far, out_ref):
    n_z, tokens, _ = own.shape
    columns = weight_ref.shape[3]
    chans = columns // 3
    count = chans // BLOCKS

    def store(slot, turned):
        for block in range(BLOCKS):
            out_ref[block, slot * count : (slot + 1) * count] = turned[
                block * count : (block + 1) * count
            ]

    total = jnp.zeros((tokens, columns), F32)
    for z in range(n_z):
        total = total + jnp.dot(
            side_by_side(own, right, far[z], left, z),
            weight_ref[z].reshape((-1, columns)),
            preferred_element_type=F32,
        )
    for which in range(3):
        store(which, total[:, which * chans : (which + 1) * chans].T)


def project_grad_kernel(weight_ref, own, left, right, far, given_ref, out_ref):
    n_z, tokens, _ = own.shape
    wide = weight_ref.shape[1] // n_z
    total = jnp.zeros((weight_ref.shape[0], tokens), F32)
    for z in range(n_z):
        total = total + lax.dot_general(
            weight_ref[:, z * wide : (z + 1) * wide],
            side_by_side(own, right, far[z], left, z),
            (((1,), (1,)), ((), ())),
            preferred_element_type=F32,
        )
    count = out_ref.shape[1] // 4
    out_ref[:, : 3 * count] = given_ref[...]
    out_ref[:, 3 * count :] = total.reshape((BLOCKS, count, tokens))


def partial_kernel(
    place_ref,
    out_hbm,
    in_weight_ref,
    channels_ref,
    own_ref,
    right_ref,
    left_ref,
    keep_r_ref,
    keep_l_ref,
    out_weight_ref,
    out_sems,
):
    n_z, _, feats, tokens = own_ref.shape
    half = n_z // 2
    ring = out_sems.shape[0]
    weight_copies = out_weight_copies(place_ref, out_hbm, out_weight_ref, out_sems)
    count = channels_ref.shape[1] // 4
    second, *grads = [
        channels_ref[:, slot * count : (slot + 1) * count].reshape((BLOCKS * count, tokens))
        for slot in range(4)
    ]
    second = second.astype(F32).T.astype(BF16)
    grads = jnp.concatenate(grads, axis=0)
    wide = out_weight_ref.shape[1] // n_z
    columns = in_weight_ref.shape[3]

    def mixed(z):
        for copy in weight_copies[z * ring : (z + 1) * ring]:
            copy.wait()
        product = jnp.dot(
            second, out_weight_ref[:, z * wide : (z + 1) * wide], preferred_element_type=F32
        )
        return [product[:, at : at + feats].astype(BF16) for at in range(0, wide, feats)]

    def token_grad(z):
        product = jnp.dot(
            in_weight_ref[z].reshape((-1, columns)), grads, preferred_element_type=F32
        )
        return [product[at : at + feats].astype(BF16) for at in range(0, wide, feats)]

    for output, pieces in ((1, token_grad), (0, mixed)):
        for z in range(n_z):
            own, ahead, far, behind = pieces(z)
            own_ref[z, output] = own
            if z < half:
                right_ref[z, output] = far
                keep_r_ref[z, output] = ahead
                left_ref[z, output] = behind
            else:
                right_ref[z, output] = ahead
                left_ref[z, output] = far
                keep_l_ref[z - half, output] = behind


def merge_kernel(keep_r_ref, keep_l_ref, from_l_ref, from_r_ref, right_ref, left_ref):
    half = keep_r_ref.shape[0]
    right_ref[...] = (keep_r_ref[...].astype(F32) + from_l_ref[:half].astype(F32)).astype(BF16)
    left_ref[...] = (keep_l_ref[...].astype(F32) + from_r_ref[half:].astype(F32)).astype(BF16)


def ring_sum_kernel(own_ref, from_l_ref, from_r_ref, last_l_ref, last_r_ref, out_ref):
    half = last_l_ref.shape[0]
    own_low, own_high = own_ref[:half].astype(F32), own_ref[half:].astype(F32)
    out_ref[:half] = (
        own_low + last_l_ref[...].astype(F32) + from_r_ref[:half].astype(F32)
    ).astype(BF16)
    out_ref[half:] = (
        own_high + from_l_ref[half:].astype(F32) + last_r_ref[...].astype(F32)
    ).astype(BF16)


def last_sum_kernel(parts_ref, mixed_ref, token_grad_ref):
    totals = []
    for output in range(2):
        total = parts_ref[0, output].astype(F32)
        for part in range(1, parts_ref.shape[0]):
            total = total + parts_ref[part, output].astype(F32)
        totals.append(total)
    mixed_ref[...] = totals[0].astype(BF16)
    token_grad_ref[...] = totals[1].T.astype(BF16)


def run(kernel, out_shape, *args, flops=0, place=None, far=(), scratch=()):
    single = not isinstance(out_shape, (list, tuple))
    outs = (out_shape,) if single else out_shape
    in_vmem = pl.BlockSpec(memory_space=pltpu.VMEM)
    places = () if place is None else (place,)
    specs = [
        *[pl.BlockSpec(memory_space=pltpu.SMEM)] * len(places),
        *[pl.BlockSpec(memory_space=pltpu.HBM)] * len(far),
        *[in_vmem] * len(args),
    ]
    held = (pltpu.with_memory_space_constraint(array, pltpu.HBM) for array in far)
    args = (*places, *held, *args)
    moved = sum(int(np.prod(a.shape)) * a.dtype.itemsize for a in (*args, *outs))
    return pl.pallas_call(
        kernel,
        out_shape=out_shape,
        in_specs=specs,
        out_specs=in_vmem if single else [in_vmem] * len(outs),
        scratch_shapes=scratch,
        compiler_params=pltpu.CompilerParams(vmem_limit_bytes=24 << 20),
        cost_estimate=pl.CostEstimate(flops=flops, bytes_accessed=moved, transcendentals=0),
    )(*args)


def shape_of(shape, dtype):
    return jax.ShapeDtypeStruct(shape, dtype)


def exchanged(value, axis):
    return lax.all_to_all(value, axis, 0, 0, tiled=True)


def shifted(value, steps):
    ring = lax.axis_size("x")
    return lax.ppermute(value, "x", [(at, (at + steps) % ring) for at in range(ring)])


def after(value, *others):
    return lax.optimization_barrier((value, *others))[0]


def on_device(tokens, in_weight, short_kernel, filters, skip_gain, out_weight, cotangent):
    width, _, chans = in_weight.shape
    rows = tokens.shape[0]
    n_z, ring = lax.axis_size("z"), lax.axis_size("x")
    half = n_z // 2
    count = chans // BLOCKS
    seq_place = lax.axis_index(SEQ).reshape((1,)).astype(jnp.int32)
    place = lax.axis_index("x").reshape((1,)).astype(jnp.int32)
    table = jnp.asarray(fine_table())
    twiddles = jnp.asarray(twiddle_table())
    split_in = in_weight.transpose((1, 0, 2)).reshape((3, n_z, ring, LANES, chans))

    sent = run(
        copies_kernel,
        shape_of((n_z, 2, rows, LANES), BF16),
        far=(tokens, cotangent),
        scratch=[pltpu.VMEM((2, rows, LANES), BF16), pltpu.SemaphoreType.DMA((2,))],
    )
    both = exchanged(sent, "z")
    one = shape_of((n_z, rows, LANES), BF16)
    own_rows, own_grads = run(apart_kernel, (one, one), both)
    left_rows = shifted(own_rows, 1)
    right_rows = shifted(own_rows, -1)
    left_grads = shifted(own_grads, 1)
    right_grads = shifted(own_grads, -1)
    far_rows = shifted(left_rows, 1)
    far_grads = shifted(right_grads, -1)

    turned_filters = run(
        turned_filters_kernel, shape_of((BLOCKS, 2 * count, rows), F32), after(filters, own_rows)
    )
    turned_filters = exchanged(turned_filters, SEQ)
    weight_sems = pltpu.SemaphoreType.DMA((ring, n_z))
    in_turned, out_turned = run(
        weights_kernel,
        (shape_of((n_z, ring, LANES, 3 * chans), BF16), shape_of(out_weight.shape, BF16)),
        far=(after(split_in, own_rows), out_weight),
        place=place,
        scratch=[pltpu.SemaphoreType.DMA((ring, 3)), weight_sems],
    )
    given = run(
        project_kernel,
        shape_of((BLOCKS, 3 * count, rows), F32),
        in_turned,
        own_rows,
        left_rows,
        right_rows,
        far_rows,
        flops=2 * rows * width * 3 * chans,
    )
    given = run(
        project_grad_kernel,
        shape_of((BLOCKS, 4 * count, rows), F32),
        out_turned,
        own_grads,
        left_grads,
        right_grads,
        far_grads,
        given,
        flops=2 * rows * width * chans,
    )
    channels = run(
        operator_kernel,
        shape_of((BLOCKS, 4 * count, LANES), BF16),
        exchanged(given, SEQ),
        turned_filters,
        place=seq_place,
        far=(table, twiddles, short_kernel, skip_gain),
        scratch=[
            pltpu.VMEM(table.shape, BF16),
            pltpu.VMEM(twiddles.shape, F32),
            pltpu.VMEM(short_kernel.shape, F32),
            pltpu.VMEM(skip_gain.shape, F32),
            pltpu.VMEM((16, chans), F32),
            pltpu.VMEM((chans, 16), F32),
            pltpu.VMEM((11, count, LANES), F32),
            pltpu.SemaphoreType.DMA((4, 1)),
        ],
    )
    whole, part = (n_z, 2, LANES, rows), (half, 2, LANES, rows)
    own, to_right, to_left, keep_r, keep_l = run(
        partial_kernel,
        tuple(shape_of(shape, BF16) for shape in (whole, whole, whole, part, part)),
        in_turned,
        exchanged(channels, SEQ),
        flops=2 * rows * width * 4 * chans,
        place=place,
        far=(out_weight,),
        scratch=[pltpu.VMEM(out_weight.shape, BF16), weight_sems],
    )
    from_l, from_r = shifted(to_right, 1), shifted(to_left, -1)
    to_right, to_left = run(
        merge_kernel, (shape_of(part, BF16), shape_of(part, BF16)), keep_r, keep_l, from_l, from_r
    )
    last_l, last_r = shifted(to_right, 1), shifted(to_left, -1)
    parts = run(ring_sum_kernel, shape_of(whole, BF16), own, from_l, from_r, last_l, last_r)
    out = shape_of((rows, LANES), BF16)
    return run(last_sum_kernel, (out, out), exchanged(parts, "z"))


def solution(mesh):
    split = Mesh(mesh.devices.reshape((4, 2, 8, 4)), ("y", "core", "z", "x"))
    chan = ("z", "x")
    in_specs = (
        P(SEQ, chan),
        P(None, None, chan),
        P(None, None, chan),
        P(None, SEQ, chan),
        P(None, chan),
        P(chan, None),
        P(SEQ, chan),
    )
    out_specs = (P(SEQ, chan), P(SEQ, chan))

    return jax.shard_map(
        on_device, mesh=split, in_specs=in_specs, out_specs=out_specs, check_vma=False
    )
```

```python
import functools
import math

import jax
import jax.numpy as jnp
import numpy as np
from jax import lax
from jax.experimental import pallas as pl
from jax.experimental.pallas import tpu as pltpu
from jax.sharding import Mesh, PartitionSpec as P


F32 = jnp.float32
BF16 = jnp.bfloat16
LANES = 128
BLOCKS = 8
COARSE = 2 * BLOCKS
KEPT = COARSE // 2 + 1
SEQ = ("y", "core")
NEAR_FIRST = (0, 1, 3, 2)


def fine_table():
    ids = np.arange(LANES)
    angle = 2.0 * np.pi / LANES * (ids[:, None] * ids[None, :] % LANES)
    table = np.stack([np.cos(angle), np.sin(angle)]).astype(np.float32)
    high = table.astype(jnp.bfloat16)
    low = (table - high.astype(np.float32)).astype(jnp.bfloat16)
    return np.stack([high, low])


def fine_matrices(table_ref):
    found = []
    for part in range(2):
        cosine, sine = table_ref[part, 0], table_ref[part, 1]
        upper = jnp.concatenate([cosine, -sine], axis=1)
        found.append(jnp.concatenate([upper, jnp.concatenate([sine, cosine], axis=1)], axis=0))
    return found


def twiddle_table():
    angle = (
        2.0 * np.pi / (COARSE * LANES) * (np.arange(KEPT)[:, None] * np.arange(LANES)[None, :])
    )
    return np.stack([np.cos(angle), np.sin(angle)]).astype(np.float32)


def coarse(index):
    index = index % COARSE
    cosine = math.cos(2.0 * math.pi * index / COARSE)
    sine = math.sin(2.0 * math.pi * index / COARSE)
    return cosine, sine


def add_term(total, value, factor):
    if abs(factor) < 1e-9:
        return total
    if abs(abs(factor) - 1.0) < 1e-9:
        if total is None:
            return value if factor > 0 else -value
        return total + value if factor > 0 else total - value
    return value * factor if total is None else total + value * factor


def precise_dot(value, matrices):
    high = value.astype(BF16)
    low = (value - high.astype(F32)).astype(BF16)
    dot = functools.partial(jnp.dot, preferred_element_type=F32)
    return (dot(low, matrices[0]) + dot(high, matrices[1])) + dot(high, matrices[0])


def spectrum(signal, matrices, twiddle_ref):
    parts = []
    for freq in range(KEPT):
        real = imag = None
        for block in range(BLOCKS):
            cosine, sine = coarse(block * freq)
            real = add_term(real, signal[block], cosine)
            imag = add_term(imag, signal[block], -sine)
        cos_t = twiddle_ref[0, freq : freq + 1, :]
        sin_t = twiddle_ref[1, freq : freq + 1, :]
        if imag is None:
            turned = (real * cos_t, -real * sin_t)
        else:
            turned = (real * cos_t + imag * sin_t, imag * cos_t - real * sin_t)
        parts.append(jnp.concatenate(turned, axis=1))
    return precise_dot(jnp.concatenate(parts, axis=0), matrices)


def restore(turned_spec, matrices, twiddle_ref):
    rows = turned_spec.shape[0] // KEPT
    back = precise_dot(turned_spec, matrices)
    real, imag = [], []
    for freq in range(KEPT):
        piece = back[freq * rows : (freq + 1) * rows]
        re, minus_im = piece[:, :LANES], piece[:, LANES:]
        cos_t = twiddle_ref[0, freq : freq + 1, :]
        sin_t = twiddle_ref[1, freq : freq + 1, :]
        real.append(re * cos_t + minus_im * sin_t)
        imag.append(re * sin_t - minus_im * cos_t)
    out = []
    for block in range(BLOCKS):
        total = None
        for freq in range(1, KEPT - 1):
            cosine, sine = coarse(block * freq)
            total = add_term(total, real[freq], cosine)
            total = add_term(total, imag[freq], -sine)
        total = 2.0 * total + real[0]
        out.append(add_term(total, real[KEPT - 1], 1.0 if block % 2 == 0 else -1.0))
    return out


def turned_product(left, right, conjugate):
    left_re, left_im = left[:, :LANES], left[:, LANES:]
    right_re, right_im = right[:, :LANES], right[:, LANES:]
    straight, crossed = left_re * right_re, left_im * right_im
    if conjugate:
        real, minus_imag = straight + crossed, left_re * right_im - left_im * right_re
    else:
        real, minus_imag = straight - crossed, -(left_re * right_im + left_im * right_re)
    return jnp.concatenate([real, minus_imag], axis=1)


def lagged(blocks, steps):
    lane = lax.broadcasted_iota(jnp.int32, blocks[0].shape, 1)
    turned = [pltpu.roll(block, steps, 1) for block in blocks]
    before = [jnp.zeros_like(blocks[0])] + turned[:-1]
    return [jnp.where(lane >= steps, own, prior) for own, prior in zip(turned, before)]


def leading(blocks, steps):
    lane = lax.broadcasted_iota(jnp.int32, blocks[0].shape, 1)
    turned = [pltpu.roll(block, LANES - steps, 1) for block in blocks]
    after = turned[1:] + [jnp.zeros_like(blocks[0])]
    return [jnp.where(lane < LANES - steps, own, later) for own, later in zip(turned, after)]


def short_sum(blocks, coef_ref, which, shift):
    total = [coef_ref[which] * block for block in blocks]
    for tap in (1, 2):
        factor = coef_ref[3 * tap + which]
        total = [have + factor * block for have, block in zip(total, shift(blocks, tap))]
    return total


def operator_kernel(
    place_ref,
    table_hbm,
    twiddle_hbm,
    taps_hbm,
    gains_hbm,
    given_ref,
    filter_ref,
    out_ref,
    table_ref,
    twiddle_ref,
    taps_ref,
    gains_ref,
    rows_ref,
    turned_ref,
    coef_ref,
    sems,
):
    count = given_ref.shape[1] // 4
    tables_in = [
        *started([table_hbm], [table_ref], sems.at[0]),
        *started([twiddle_hbm], [twiddle_ref], sems.at[1]),
    ]
    coef_in = [
        *started([taps_hbm], [taps_ref], sems.at[2]),
        *started([gains_hbm], [gains_ref], sems.at[3]),
    ]
    for copy in coef_in:
        copy.wait()
    rows_ref[...] = jnp.zeros_like(rows_ref)
    for tap in range(3):
        for which in range(3):
            rows_ref[3 * tap + which] = taps_ref[tap, which]
    for order in range(2):
        rows_ref[9 + order] = gains_ref[order]
    turned_ref[...] = rows_ref[...].T
    own_start = pl.multiple_of(place_ref[0] * count, count)
    columns = turned_ref[pl.ds(own_start, count), :]
    for at in range(coef_ref.shape[0]):
        coef_ref[at] = jnp.broadcast_to(columns[:, at : at + 1], coef_ref.shape[1:])

    def rows_of(slot, ref=given_ref):
        return [ref[block, slot * count : (slot + 1) * count] for block in range(BLOCKS)]

    def store(slot, blocks):
        for block, value in enumerate(blocks):
            out_ref[block, slot * count : (slot + 1) * count] = value.astype(BF16)

    def scaled(gain, blocks):
        return [coef_ref[gain] * value for value in blocks]

    def product(left, right):
        return [one * two for one, two in zip(left, right)]

    def plus(left, right):
        return [one + two for one, two in zip(left, right)]

    def filtered(blocks, order, conjugate):
        spec = turned_product(
            spectrum(blocks, matrices, twiddle_ref), filter_spec[order], conjugate
        )
        return plus(restore(spec, matrices, twiddle_ref), scaled(9 + order, blocks))

    values = short_sum(rows_of(0), coef_ref, 0, lagged)
    gate_one = short_sum(rows_of(1), coef_ref, 1, lagged)
    gate_two = short_sum(rows_of(2), coef_ref, 2, lagged)
    for copy in tables_in:
        copy.wait()
    matrices = fine_matrices(table_ref)
    filter_spec = [
        spectrum(rows_of(order, filter_ref), matrices, twiddle_ref) * (1.0 / (COARSE * LANES))
        for order in range(2)
    ]
    conv_one = filtered(values, 0, False)
    conv_two = filtered(product(gate_one, conv_one), 1, False)
    store(0, product(gate_two, conv_two))
    grad_two = rows_of(3)
    store(3, short_sum(product(grad_two, conv_two), coef_ref, 2, leading))
    grad_first = filtered(product(grad_two, gate_two), 1, True)
    store(2, short_sum(product(grad_first, conv_one), coef_ref, 1, leading))
    grad_values = filtered(product(grad_first, gate_one), 0, True)
    store(1, short_sum(grad_values, coef_ref, 0, leading))


def started(source_refs, targets, sems):
    found = []
    for at, (source, target) in enumerate(zip(source_refs, targets)):
        copy = pltpu.make_async_copy(source, target, sems.at[at])
        copy.start()
        found.append(copy)
    return found


def copies_kernel(tokens_hbm, cotangent_hbm, out_ref, held, sems):
    begun = started([tokens_hbm, cotangent_hbm], [held.at[0], held.at[1]], sems)
    for copy in begun:
        copy.wait()
    for at in range(out_ref.shape[0]):
        out_ref[at] = held[...]


def halves_kernel(left_hbm, right_hbm, low_ref, high_ref, sems):
    half = low_ref.shape[0]
    sources = [left_hbm.at[pl.ds(0, half)], right_hbm.at[pl.ds(half, half)]]
    for copy in started(sources, [low_ref, high_ref], sems):
        copy.wait()


def turned_filters_kernel(filter_ref, out_ref):
    count = out_ref.shape[1] // 2
    for order in range(2):
        turned = filter_ref[order].T
        for block in range(BLOCKS):
            out_ref[block, order * count : (order + 1) * count] = turned[
                block * count : (block + 1) * count
            ]


def weights_kernel(place_ref, in_hbm, in_ref, sems):
    parts, _, ring, _, chans = in_hbm.shape
    begun = []
    for slot, apart in enumerate(NEAR_FIRST):
        source = lax.rem(place_ref[0] + apart, ring)
        for part in range(parts):
            copy = pltpu.make_async_copy(
                in_hbm.at[part, :, source],
                in_ref.at[:, slot, :, pl.ds(part * chans, chans)],
                sems.at[slot, part],
            )
            copy.start()
            begun.append(copy)
    for copy in begun:
        copy.wait()


def ring_columns(place_ref, weight_ref, ring, feats, z):
    found = []
    for apart in NEAR_FIRST:
        block = z * ring + lax.rem(place_ref[0] + apart, ring)
        found.append(weight_ref[:, pl.ds(pl.multiple_of(block * feats, feats), feats)])
    return jnp.concatenate(found, axis=1)


def near_kernel(
    place_ref,
    out_hbm,
    weight_ref,
    own,
    left,
    right,
    rows_ref,
    grads_ref,
    far_weight_ref,
    out_weight_ref,
    sems,
):
    (weight_copy,) = started([out_hbm], [out_weight_ref], sems)
    n_z, _, tokens, feats = own.shape
    ring, columns = weight_ref.shape[1], weight_ref.shape[3]

    def near(which, z):
        return jnp.concatenate([ref[z, which] for ref in (own, right, left)], axis=1)

    total = jnp.zeros((tokens, columns), F32)
    for z in range(n_z):
        total = total + jnp.dot(
            near(0, z),
            weight_ref[z, : ring - 1].reshape((-1, columns)),
            preferred_element_type=F32,
        )
    rows_ref[...] = total
    weight_copy.wait()
    total = jnp.zeros((out_weight_ref.shape[0], tokens), F32)
    for z in range(n_z):
        turned = ring_columns(place_ref, out_weight_ref, ring, feats, z)
        far_weight_ref[z] = turned[:, (ring - 1) * feats :]
        total = total + lax.dot_general(
            turned[:, : (ring - 1) * feats],
            near(1, z),
            (((1,), (1,)), ((), ())),
            preferred_element_type=F32,
        )
    grads_ref[...] = total


def far_kernel(weight_ref, far_weight_ref, rows_ref, grads_ref, low, high, out_ref):
    n_z, last = weight_ref.shape[0], weight_ref.shape[1] - 1
    half = low.shape[0]
    chans = far_weight_ref.shape[1]
    count = chans // BLOCKS
    rows, grads = rows_ref[...], grads_ref[...]
    for z in range(n_z):
        far = low.at[z] if z < half else high.at[z - half]
        rows = rows + jnp.dot(far[0], weight_ref[z, last], preferred_element_type=F32)
        grads = grads + lax.dot_general(
            far_weight_ref[z], far[1], (((1,), (1,)), ((), ())), preferred_element_type=F32
        )

    def store(slot, turned):
        for block in range(BLOCKS):
            out_ref[block, slot * count : (slot + 1) * count] = turned[
                block * count : (block + 1) * count
            ]

    for which in range(3):
        store(which, rows[:, which * chans : (which + 1) * chans].T)
    store(3, grads)


def partial_kernel(
    place_ref,
    out_hbm,
    in_weight_ref,
    channels_ref,
    own_ref,
    right_ref,
    left_ref,
    keep_r_ref,
    keep_l_ref,
    out_weight_ref,
    sems,
):
    n_z, _, feats, tokens = own_ref.shape
    half = n_z // 2
    ring = in_weight_ref.shape[1]
    (weight_copy,) = started([out_hbm], [out_weight_ref], sems)
    count = channels_ref.shape[1] // 4
    second, *grads = [
        channels_ref[:, slot * count : (slot + 1) * count].reshape((BLOCKS * count, tokens))
        for slot in range(4)
    ]
    second = second.astype(F32).T.astype(BF16)
    grads = jnp.concatenate(grads, axis=0)
    wide = out_weight_ref.shape[1] // n_z
    columns = in_weight_ref.shape[3]

    def mixed(z):
        product = jnp.dot(
            second,
            ring_columns(place_ref, out_weight_ref, ring, feats, z),
            preferred_element_type=F32,
        )
        return [product[:, at : at + feats].astype(BF16) for at in range(0, wide, feats)]

    def token_grad(z):
        product = jnp.dot(
            in_weight_ref[z].reshape((-1, columns)), grads, preferred_element_type=F32
        )
        return [product[at : at + feats].astype(BF16) for at in range(0, wide, feats)]

    for output, pieces in ((1, token_grad), (0, mixed)):
        if output == 0:
            weight_copy.wait()
        for z in range(n_z):
            own, ahead, behind, far = pieces(z)
            own_ref[z, output] = own
            if z < half:
                right_ref[z, output] = far
                keep_r_ref[z, output] = ahead
                left_ref[z, output] = behind
            else:
                right_ref[z, output] = ahead
                left_ref[z, output] = far
                keep_l_ref[z - half, output] = behind


def merge_kernel(keep_r_ref, keep_l_ref, from_l_ref, from_r_ref, right_ref, left_ref):
    half = keep_r_ref.shape[0]
    right_ref[...] = (keep_r_ref[...].astype(F32) + from_l_ref[:half].astype(F32)).astype(BF16)
    left_ref[...] = (keep_l_ref[...].astype(F32) + from_r_ref[half:].astype(F32)).astype(BF16)


def ring_sum_kernel(own_ref, from_l_ref, from_r_ref, last_l_ref, last_r_ref, out_ref):
    half = last_l_ref.shape[0]
    own_low, own_high = own_ref[:half].astype(F32), own_ref[half:].astype(F32)
    out_ref[:half] = (
        own_low + last_l_ref[...].astype(F32) + from_r_ref[:half].astype(F32)
    ).astype(BF16)
    out_ref[half:] = (
        own_high + from_l_ref[half:].astype(F32) + last_r_ref[...].astype(F32)
    ).astype(BF16)


def last_sum_kernel(parts_ref, mixed_ref, token_grad_ref):
    totals = []
    for output in range(2):
        total = parts_ref[0, output].astype(F32)
        for part in range(1, parts_ref.shape[0]):
            total = total + parts_ref[part, output].astype(F32)
        totals.append(total)
    mixed_ref[...] = totals[0].astype(BF16)
    token_grad_ref[...] = totals[1].T.astype(BF16)


def run(kernel, out_shape, *args, flops=0, place=None, far=(), scratch=()):
    single = not isinstance(out_shape, (list, tuple))
    outs = (out_shape,) if single else out_shape
    in_vmem = pl.BlockSpec(memory_space=pltpu.VMEM)
    places = () if place is None else (place,)
    specs = [
        *[pl.BlockSpec(memory_space=pltpu.SMEM)] * len(places),
        *[pl.BlockSpec(memory_space=pltpu.HBM)] * len(far),
        *[in_vmem] * len(args),
    ]
    held = (pltpu.with_memory_space_constraint(array, pltpu.HBM) for array in far)
    args = (*places, *held, *args)
    moved = sum(int(np.prod(a.shape)) * a.dtype.itemsize for a in (*args, *outs))
    return pl.pallas_call(
        kernel,
        out_shape=out_shape,
        in_specs=specs,
        out_specs=in_vmem if single else [in_vmem] * len(outs),
        scratch_shapes=scratch,
        compiler_params=pltpu.CompilerParams(vmem_limit_bytes=24 << 20),
        cost_estimate=pl.CostEstimate(flops=flops, bytes_accessed=moved, transcendentals=0),
    )(*args)


def shape_of(shape, dtype):
    return jax.ShapeDtypeStruct(shape, dtype)


def exchanged(value, axis):
    return lax.all_to_all(value, axis, 0, 0, tiled=True)


def shifted(value, steps):
    ring = lax.axis_size("x")
    return lax.ppermute(value, "x", [(at, (at + steps) % ring) for at in range(ring)])


def after(value, *others):
    return lax.optimization_barrier((value, *others))[0]


def on_device(tokens, in_weight, short_kernel, filters, skip_gain, out_weight, cotangent):
    width, _, chans = in_weight.shape
    rows = tokens.shape[0]
    n_z, ring = lax.axis_size("z"), lax.axis_size("x")
    half = n_z // 2
    count = chans // BLOCKS
    seq_place = lax.axis_index(SEQ).reshape((1,)).astype(jnp.int32)
    place = lax.axis_index("x").reshape((1,)).astype(jnp.int32)
    table = jnp.asarray(fine_table())
    twiddles = jnp.asarray(twiddle_table())
    split_in = in_weight.transpose((1, 0, 2)).reshape((3, n_z, ring, LANES, chans))

    sent = run(
        copies_kernel,
        shape_of((n_z, 2, rows, LANES), BF16),
        far=(tokens, cotangent),
        scratch=[pltpu.VMEM((2, rows, LANES), BF16), pltpu.SemaphoreType.DMA((2,))],
    )
    both = exchanged(sent, "z")
    left, right = shifted(both, 1), shifted(both, -1)
    some = shape_of((half, 2, rows, LANES), BF16)
    low, high = run(
        halves_kernel, (some, some), far=(left, right), scratch=[pltpu.SemaphoreType.DMA((2,))]
    )
    low, high = shifted(low, 1), shifted(high, -1)

    turned_filters = run(
        turned_filters_kernel, shape_of((BLOCKS, 2 * count, rows), F32), after(filters, both)
    )
    turned_filters = exchanged(turned_filters, SEQ)
    in_turned = run(
        weights_kernel,
        shape_of((n_z, ring, LANES, 3 * chans), BF16),
        far=(after(split_in, both),),
        place=place,
        scratch=[pltpu.SemaphoreType.DMA((ring, 3))],
    )
    out_scratch = [pltpu.VMEM(out_weight.shape, BF16), pltpu.SemaphoreType.DMA((1,))]
    *near, far_weight = run(
        near_kernel,
        (
            shape_of((rows, 3 * chans), F32),
            shape_of((chans, rows), F32),
            shape_of((n_z, chans, LANES), BF16),
        ),
        in_turned,
        both,
        left,
        right,
        flops=2 * rows * width * 3 * chans,
        place=place,
        far=(out_weight,),
        scratch=out_scratch,
    )
    given = run(
        far_kernel,
        shape_of((BLOCKS, 4 * count, rows), F32),
        in_turned,
        far_weight,
        *near,
        low,
        high,
        flops=2 * rows * width * chans,
    )
    channels = run(
        operator_kernel,
        shape_of((BLOCKS, 4 * count, LANES), BF16),
        exchanged(given, SEQ),
        turned_filters,
        place=seq_place,
        far=(table, twiddles, short_kernel, skip_gain),
        scratch=[
            pltpu.VMEM(table.shape, BF16),
            pltpu.VMEM(twiddles.shape, F32),
            pltpu.VMEM(short_kernel.shape, F32),
            pltpu.VMEM(skip_gain.shape, F32),
            pltpu.VMEM((16, chans), F32),
            pltpu.VMEM((chans, 16), F32),
            pltpu.VMEM((11, count, LANES), F32),
            pltpu.SemaphoreType.DMA((4, 1)),
        ],
    )
    whole, part = (n_z, 2, LANES, rows), (half, 2, LANES, rows)
    own, to_right, to_left, keep_r, keep_l = run(
        partial_kernel,
        tuple(shape_of(shape, BF16) for shape in (whole, whole, whole, part, part)),
        in_turned,
        exchanged(channels, SEQ),
        flops=2 * rows * width * 4 * chans,
        place=place,
        far=(out_weight,),
        scratch=out_scratch,
    )
    from_l, from_r = shifted(to_right, 1), shifted(to_left, -1)
    to_right, to_left = run(
        merge_kernel, (shape_of(part, BF16), shape_of(part, BF16)), keep_r, keep_l, from_l, from_r
    )
    last_l, last_r = shifted(to_right, 1), shifted(to_left, -1)
    parts = run(ring_sum_kernel, shape_of(whole, BF16), own, from_l, from_r, last_l, last_r)
    out = shape_of((rows, LANES), BF16)
    return run(last_sum_kernel, (out, out), exchanged(parts, "z"))


def solution(mesh):
    split = Mesh(mesh.devices.reshape((4, 2, 8, 4)), ("y", "core", "z", "x"))
    chan = ("z", "x")
    in_specs = (
        P(SEQ, chan),
        P(None, None, chan),
        P(None, None, chan),
        P(None, SEQ, chan),
        P(None, chan),
        P(chan, None),
        P(SEQ, chan),
    )
    out_specs = (P(SEQ, chan), P(SEQ, chan))

    return jax.shard_map(
        on_device, mesh=split, in_specs=in_specs, out_specs=out_specs, check_vma=False
    )
```

```python
import functools
import math

import jax
import jax.numpy as jnp
import numpy as np
from jax import lax
from jax.experimental import pallas as pl
from jax.experimental.pallas import tpu as pltpu
from jax.sharding import Mesh, PartitionSpec as P


F32 = jnp.float32
BF16 = jnp.bfloat16
LANES = 128
BLOCKS = 8
COARSE = 2 * BLOCKS
KEPT = COARSE // 2 + 1
SEQ = ("y", "core")
NEAR_FIRST = (0, 1, 3, 2)


def fine_table():
    ids = np.arange(LANES)
    angle = 2.0 * np.pi / LANES * (ids[:, None] * ids[None, :] % LANES)
    table = np.stack([np.cos(angle), np.sin(angle)]).astype(np.float32)
    high = table.astype(jnp.bfloat16)
    low = (table - high.astype(np.float32)).astype(jnp.bfloat16)
    return np.stack([high, low])


def fine_matrices(table_ref):
    found = []
    for part in range(2):
        cosine, sine = table_ref[part, 0], table_ref[part, 1]
        upper = jnp.concatenate([cosine, -sine], axis=1)
        found.append(jnp.concatenate([upper, jnp.concatenate([sine, cosine], axis=1)], axis=0))
    return found


def twiddle_table():
    angle = (
        2.0 * np.pi / (COARSE * LANES) * (np.arange(KEPT)[:, None] * np.arange(LANES)[None, :])
    )
    return np.stack([np.cos(angle), np.sin(angle)]).astype(np.float32)


def coarse(index):
    index = index % COARSE
    cosine = math.cos(2.0 * math.pi * index / COARSE)
    sine = math.sin(2.0 * math.pi * index / COARSE)
    return cosine, sine


def add_term(total, value, factor):
    if abs(factor) < 1e-9:
        return total
    if abs(abs(factor) - 1.0) < 1e-9:
        if total is None:
            return value if factor > 0 else -value
        return total + value if factor > 0 else total - value
    return value * factor if total is None else total + value * factor


def precise_dot(value, matrices):
    high = value.astype(BF16)
    low = (value - high.astype(F32)).astype(BF16)
    dot = functools.partial(jnp.dot, preferred_element_type=F32)
    return (dot(low, matrices[0]) + dot(high, matrices[1])) + dot(high, matrices[0])


def spectrum(signal, matrices, twiddle_ref):
    parts = []
    for freq in range(KEPT):
        real = imag = None
        for block in range(BLOCKS):
            cosine, sine = coarse(block * freq)
            real = add_term(real, signal[block], cosine)
            imag = add_term(imag, signal[block], -sine)
        cos_t = twiddle_ref[0, freq : freq + 1, :]
        sin_t = twiddle_ref[1, freq : freq + 1, :]
        if imag is None:
            turned = (real * cos_t, -real * sin_t)
        else:
            turned = (real * cos_t + imag * sin_t, imag * cos_t - real * sin_t)
        parts.append(jnp.concatenate(turned, axis=1))
    return precise_dot(jnp.concatenate(parts, axis=0), matrices)


def restore(turned_spec, matrices, twiddle_ref):
    rows = turned_spec.shape[0] // KEPT
    back = precise_dot(turned_spec, matrices)
    real, imag = [], []
    for freq in range(KEPT):
        piece = back[freq * rows : (freq + 1) * rows]
        re, minus_im = piece[:, :LANES], piece[:, LANES:]
        cos_t = twiddle_ref[0, freq : freq + 1, :]
        sin_t = twiddle_ref[1, freq : freq + 1, :]
        real.append(re * cos_t + minus_im * sin_t)
        imag.append(re * sin_t - minus_im * cos_t)
    out = []
    for block in range(BLOCKS):
        total = None
        for freq in range(1, KEPT - 1):
            cosine, sine = coarse(block * freq)
            total = add_term(total, real[freq], cosine)
            total = add_term(total, imag[freq], -sine)
        total = 2.0 * total + real[0]
        out.append(add_term(total, real[KEPT - 1], 1.0 if block % 2 == 0 else -1.0))
    return out


def turned_product(left, right, conjugate):
    left_re, left_im = left[:, :LANES], left[:, LANES:]
    right_re, right_im = right[:, :LANES], right[:, LANES:]
    straight, crossed = left_re * right_re, left_im * right_im
    if conjugate:
        real, minus_imag = straight + crossed, left_re * right_im - left_im * right_re
    else:
        real, minus_imag = straight - crossed, -(left_re * right_im + left_im * right_re)
    return jnp.concatenate([real, minus_imag], axis=1)


def lagged(blocks, steps):
    lane = lax.broadcasted_iota(jnp.int32, blocks[0].shape, 1)
    turned = [pltpu.roll(block, steps, 1) for block in blocks]
    before = [jnp.zeros_like(blocks[0])] + turned[:-1]
    return [jnp.where(lane >= steps, own, prior) for own, prior in zip(turned, before)]


def leading(blocks, steps):
    lane = lax.broadcasted_iota(jnp.int32, blocks[0].shape, 1)
    turned = [pltpu.roll(block, LANES - steps, 1) for block in blocks]
    after = turned[1:] + [jnp.zeros_like(blocks[0])]
    return [jnp.where(lane < LANES - steps, own, later) for own, later in zip(turned, after)]


def short_sum(blocks, coef_ref, which, shift):
    total = [coef_ref[which] * block for block in blocks]
    for tap in (1, 2):
        factor = coef_ref[3 * tap + which]
        total = [have + factor * block for have, block in zip(total, shift(blocks, tap))]
    return total


def operator_kernel(
    place_ref,
    table_hbm,
    twiddle_hbm,
    taps_hbm,
    gains_hbm,
    given_ref,
    filter_ref,
    out_ref,
    table_ref,
    twiddle_ref,
    taps_ref,
    gains_ref,
    rows_ref,
    turned_ref,
    coef_ref,
    sems,
):
    count = given_ref.shape[1] // 4
    tables_in = [
        *started([table_hbm], [table_ref], sems.at[0]),
        *started([twiddle_hbm], [twiddle_ref], sems.at[1]),
    ]
    coef_in = [
        *started([taps_hbm], [taps_ref], sems.at[2]),
        *started([gains_hbm], [gains_ref], sems.at[3]),
    ]
    for copy in coef_in:
        copy.wait()
    rows_ref[...] = jnp.zeros_like(rows_ref)
    for tap in range(3):
        for which in range(3):
            rows_ref[3 * tap + which] = taps_ref[tap, which]
    for order in range(2):
        rows_ref[9 + order] = gains_ref[order]
    turned_ref[...] = rows_ref[...].T
    own_start = pl.multiple_of(place_ref[0] * count, count)
    columns = turned_ref[pl.ds(own_start, count), :]
    for at in range(coef_ref.shape[0]):
        coef_ref[at] = jnp.broadcast_to(columns[:, at : at + 1], coef_ref.shape[1:])

    def rows_of(slot, ref=given_ref):
        return [ref[block, slot * count : (slot + 1) * count] for block in range(BLOCKS)]

    def store(slot, blocks):
        for block, value in enumerate(blocks):
            out_ref[block, slot * count : (slot + 1) * count] = value.astype(BF16)

    def scaled(gain, blocks):
        return [coef_ref[gain] * value for value in blocks]

    def product(left, right):
        return [one * two for one, two in zip(left, right)]

    def plus(left, right):
        return [one + two for one, two in zip(left, right)]

    def filtered(blocks, order, conjugate):
        spec = turned_product(
            spectrum(blocks, matrices, twiddle_ref), filter_spec[order], conjugate
        )
        return plus(restore(spec, matrices, twiddle_ref), scaled(9 + order, blocks))

    values = short_sum(rows_of(0), coef_ref, 0, lagged)
    gate_one = short_sum(rows_of(1), coef_ref, 1, lagged)
    gate_two = short_sum(rows_of(2), coef_ref, 2, lagged)
    for copy in tables_in:
        copy.wait()
    matrices = fine_matrices(table_ref)
    filter_spec = [
        spectrum(rows_of(order, filter_ref), matrices, twiddle_ref) * (1.0 / (COARSE * LANES))
        for order in range(2)
    ]
    conv_one = filtered(values, 0, False)
    conv_two = filtered(product(gate_one, conv_one), 1, False)
    store(0, product(gate_two, conv_two))
    grad_two = rows_of(3)
    store(3, short_sum(product(grad_two, conv_two), coef_ref, 2, leading))
    grad_first = filtered(product(grad_two, gate_two), 1, True)
    store(2, short_sum(product(grad_first, conv_one), coef_ref, 1, leading))
    grad_values = filtered(product(grad_first, gate_one), 0, True)
    store(1, short_sum(grad_values, coef_ref, 0, leading))


def started(source_refs, targets, sems):
    found = []
    for at, (source, target) in enumerate(zip(source_refs, targets)):
        copy = pltpu.make_async_copy(source, target, sems.at[at])
        copy.start()
        found.append(copy)
    return found


def copies_kernel(tokens_hbm, cotangent_hbm, out_ref, held, sems):
    begun = started([tokens_hbm, cotangent_hbm], [held.at[0], held.at[1]], sems)
    for copy in begun:
        copy.wait()
    for at in range(out_ref.shape[0]):
        out_ref[at] = held[...]


def halves_kernel(left_hbm, right_hbm, low_ref, high_ref, sems):
    half = low_ref.shape[0]
    sources = [left_hbm.at[pl.ds(0, half)], right_hbm.at[pl.ds(half, half)]]
    for copy in started(sources, [low_ref, high_ref], sems):
        copy.wait()


def turned_filters_kernel(filter_ref, out_ref):
    count = out_ref.shape[1] // 2
    for order in range(2):
        turned = filter_ref[order].T
        for block in range(BLOCKS):
            out_ref[block, order * count : (order + 1) * count] = turned[
                block * count : (block + 1) * count
            ]


def weights_kernel(place_ref, in_hbm, in_ref, sems):
    parts, _, ring, _, chans = in_hbm.shape
    begun = []
    for slot, apart in enumerate(NEAR_FIRST):
        source = lax.rem(place_ref[0] + apart, ring)
        for part in range(parts):
            copy = pltpu.make_async_copy(
                in_hbm.at[part, :, source],
                in_ref.at[:, slot, :, pl.ds(part * chans, chans)],
                sems.at[slot, part],
            )
            copy.start()
            begun.append(copy)
    for copy in begun:
        copy.wait()


def ring_columns(place_ref, weight_ref, ring, feats, z):
    found = []
    for apart in NEAR_FIRST:
        block = z * ring + lax.rem(place_ref[0] + apart, ring)
        found.append(weight_ref[:, pl.ds(pl.multiple_of(block * feats, feats), feats)])
    return jnp.concatenate(found, axis=1)


def near_kernel(
    place_ref,
    out_hbm,
    weight_ref,
    own,
    left,
    right,
    rows_ref,
    grads_ref,
    far_weight_ref,
    out_weight_ref,
    sems,
):
    (weight_copy,) = started([out_hbm], [out_weight_ref], sems)
    n_z, _, tokens, feats = own.shape
    ring, columns = weight_ref.shape[1], weight_ref.shape[3]

    def near(which, z):
        return jnp.concatenate([ref[z, which] for ref in (own, right, left)], axis=1)

    total = jnp.zeros((tokens, columns), F32)
    for z in range(n_z):
        total = total + jnp.dot(
            near(0, z),
            weight_ref[z, : ring - 1].reshape((-1, columns)),
            preferred_element_type=F32,
        )
    rows_ref[...] = total
    weight_copy.wait()
    total = jnp.zeros((out_weight_ref.shape[0], tokens), F32)
    for z in range(n_z):
        turned = ring_columns(place_ref, out_weight_ref, ring, feats, z)
        far_weight_ref[z] = turned[:, (ring - 1) * feats :]
        total = total + lax.dot_general(
            turned[:, : (ring - 1) * feats],
            near(1, z),
            (((1,), (1,)), ((), ())),
            preferred_element_type=F32,
        )
    grads_ref[...] = total


def far_kernel(weight_ref, far_weight_ref, rows_ref, grads_ref, low, high, out_ref):
    n_z, last = weight_ref.shape[0], weight_ref.shape[1] - 1
    half = low.shape[0]
    chans = far_weight_ref.shape[1]
    count = chans // BLOCKS
    rows, grads = rows_ref[...], grads_ref[...]
    for z in range(n_z):
        far = low.at[z] if z < half else high.at[z - half]
        rows = rows + jnp.dot(far[0], weight_ref[z, last], preferred_element_type=F32)
        grads = grads + lax.dot_general(
            far_weight_ref[z], far[1], (((1,), (1,)), ((), ())), preferred_element_type=F32
        )

    def store(slot, turned):
        for block in range(BLOCKS):
            out_ref[block, slot * count : (slot + 1) * count] = turned[
                block * count : (block + 1) * count
            ]

    for which in range(3):
        store(which, rows[:, which * chans : (which + 1) * chans].T)
    store(3, grads)


def partial_kernel(
    place_ref,
    out_hbm,
    in_weight_ref,
    channels_ref,
    own_ref,
    far_r_ref,
    far_l_ref,
    near_r_ref,
    near_l_ref,
    keep_r_ref,
    keep_l_ref,
    out_weight_ref,
    sems,
):
    n_z, _, feats, tokens = own_ref.shape
    half = n_z // 2
    ring = in_weight_ref.shape[1]
    (weight_copy,) = started([out_hbm], [out_weight_ref], sems)
    count = channels_ref.shape[1] // 4
    second, *grads = [
        channels_ref[:, slot * count : (slot + 1) * count].reshape((BLOCKS * count, tokens))
        for slot in range(4)
    ]
    second = second.astype(F32).T.astype(BF16)
    grads = jnp.concatenate(grads, axis=0)
    wide = out_weight_ref.shape[1] // n_z
    columns = in_weight_ref.shape[3]

    def mixed(z):
        product = jnp.dot(
            second,
            ring_columns(place_ref, out_weight_ref, ring, feats, z),
            preferred_element_type=F32,
        )
        return [product[:, at : at + feats].astype(BF16) for at in range(0, wide, feats)]

    def token_grad(z):
        product = jnp.dot(
            in_weight_ref[z].reshape((-1, columns)), grads, preferred_element_type=F32
        )
        return [product[at : at + feats].astype(BF16) for at in range(0, wide, feats)]

    for output, pieces in ((1, token_grad), (0, mixed)):
        if output == 0:
            weight_copy.wait()
        for z in range(n_z):
            own, ahead, behind, far = pieces(z)
            own_ref[z, output] = own
            if z < half:
                far_r_ref[z, output] = far
                keep_r_ref[z, output] = ahead
                near_l_ref[z, output] = behind
            else:
                near_r_ref[z - half, output] = ahead
                far_l_ref[z - half, output] = far
                keep_l_ref[z - half, output] = behind


def merge_kernel(keep_r_ref, keep_l_ref, from_l_ref, from_r_ref, right_ref, left_ref):
    right_ref[...] = (keep_r_ref[...].astype(F32) + from_l_ref[...].astype(F32)).astype(BF16)
    left_ref[...] = (keep_l_ref[...].astype(F32) + from_r_ref[...].astype(F32)).astype(BF16)


def ring_sum_kernel(own_ref, near_l_ref, near_r_ref, last_l_ref, last_r_ref, out_ref):
    half = last_l_ref.shape[0]
    own_low, own_high = own_ref[:half].astype(F32), own_ref[half:].astype(F32)
    out_ref[:half] = (
        own_low + last_l_ref[...].astype(F32) + near_r_ref[...].astype(F32)
    ).astype(BF16)
    out_ref[half:] = (
        own_high + near_l_ref[...].astype(F32) + last_r_ref[...].astype(F32)
    ).astype(BF16)


def last_sum_kernel(parts_ref, mixed_ref, token_grad_ref):
    totals = []
    for output in range(2):
        total = parts_ref[0, output].astype(F32)
        for part in range(1, parts_ref.shape[0]):
            total = total + parts_ref[part, output].astype(F32)
        totals.append(total)
    mixed_ref[...] = totals[0].astype(BF16)
    token_grad_ref[...] = totals[1].T.astype(BF16)


def run(kernel, out_shape, *args, flops=0, place=None, far=(), scratch=()):
    single = not isinstance(out_shape, (list, tuple))
    outs = (out_shape,) if single else out_shape
    in_vmem = pl.BlockSpec(memory_space=pltpu.VMEM)
    places = () if place is None else (place,)
    specs = [
        *[pl.BlockSpec(memory_space=pltpu.SMEM)] * len(places),
        *[pl.BlockSpec(memory_space=pltpu.HBM)] * len(far),
        *[in_vmem] * len(args),
    ]
    held = (pltpu.with_memory_space_constraint(array, pltpu.HBM) for array in far)
    args = (*places, *held, *args)
    moved = sum(int(np.prod(a.shape)) * a.dtype.itemsize for a in (*args, *outs))
    return pl.pallas_call(
        kernel,
        out_shape=out_shape,
        in_specs=specs,
        out_specs=in_vmem if single else [in_vmem] * len(outs),
        scratch_shapes=scratch,
        compiler_params=pltpu.CompilerParams(vmem_limit_bytes=24 << 20),
        cost_estimate=pl.CostEstimate(flops=flops, bytes_accessed=moved, transcendentals=0),
    )(*args)


def shape_of(shape, dtype):
    return jax.ShapeDtypeStruct(shape, dtype)


def exchanged(value, axis):
    return lax.all_to_all(value, axis, 0, 0, tiled=True)


def shifted(value, steps):
    ring = lax.axis_size("x")
    return lax.ppermute(value, "x", [(at, (at + steps) % ring) for at in range(ring)])


def after(value, *others):
    return lax.optimization_barrier((value, *others))[0]


def on_device(tokens, in_weight, short_kernel, filters, skip_gain, out_weight, cotangent):
    width, _, chans = in_weight.shape
    rows = tokens.shape[0]
    n_z, ring = lax.axis_size("z"), lax.axis_size("x")
    half = n_z // 2
    count = chans // BLOCKS
    seq_place = lax.axis_index(SEQ).reshape((1,)).astype(jnp.int32)
    place = lax.axis_index("x").reshape((1,)).astype(jnp.int32)
    table = jnp.asarray(fine_table())
    twiddles = jnp.asarray(twiddle_table())
    split_in = in_weight.transpose((1, 0, 2)).reshape((3, n_z, ring, LANES, chans))

    sent = run(
        copies_kernel,
        shape_of((n_z, 2, rows, LANES), BF16),
        far=(tokens, cotangent),
        scratch=[pltpu.VMEM((2, rows, LANES), BF16), pltpu.SemaphoreType.DMA((2,))],
    )
    both = exchanged(sent, "z")
    left, right = shifted(both, 1), shifted(both, -1)
    some = shape_of((half, 2, rows, LANES), BF16)
    low, high = run(
        halves_kernel, (some, some), far=(left, right), scratch=[pltpu.SemaphoreType.DMA((2,))]
    )
    low, high = shifted(low, 1), shifted(high, -1)

    turned_filters = run(
        turned_filters_kernel, shape_of((BLOCKS, 2 * count, rows), F32), after(filters, both)
    )
    turned_filters = exchanged(turned_filters, SEQ)
    in_turned = run(
        weights_kernel,
        shape_of((n_z, ring, LANES, 3 * chans), BF16),
        far=(after(split_in, both),),
        place=place,
        scratch=[pltpu.SemaphoreType.DMA((ring, 3))],
    )
    out_scratch = [pltpu.VMEM(out_weight.shape, BF16), pltpu.SemaphoreType.DMA((1,))]
    *near, far_weight = run(
        near_kernel,
        (
            shape_of((rows, 3 * chans), F32),
            shape_of((chans, rows), F32),
            shape_of((n_z, chans, LANES), BF16),
        ),
        in_turned,
        both,
        left,
        right,
        flops=2 * rows * width * 3 * chans,
        place=place,
        far=(out_weight,),
        scratch=out_scratch,
    )
    given = run(
        far_kernel,
        shape_of((BLOCKS, 4 * count, rows), F32),
        in_turned,
        far_weight,
        *near,
        low,
        high,
        flops=2 * rows * width * chans,
    )
    channels = run(
        operator_kernel,
        shape_of((BLOCKS, 4 * count, LANES), BF16),
        exchanged(given, SEQ),
        turned_filters,
        place=seq_place,
        far=(table, twiddles, short_kernel, skip_gain),
        scratch=[
            pltpu.VMEM(table.shape, BF16),
            pltpu.VMEM(twiddles.shape, F32),
            pltpu.VMEM(short_kernel.shape, F32),
            pltpu.VMEM(skip_gain.shape, F32),
            pltpu.VMEM((16, chans), F32),
            pltpu.VMEM((chans, 16), F32),
            pltpu.VMEM((11, count, LANES), F32),
            pltpu.SemaphoreType.DMA((4, 1)),
        ],
    )
    whole, part = (n_z, 2, LANES, rows), (half, 2, LANES, rows)
    own, far_r, far_l, near_r, near_l, keep_r, keep_l = run(
        partial_kernel,
        tuple(shape_of(shape, BF16) for shape in (whole, *[part] * 6)),
        in_turned,
        exchanged(channels, SEQ),
        flops=2 * rows * width * 4 * chans,
        place=place,
        far=(out_weight,),
        scratch=out_scratch,
    )
    from_l, from_r = shifted(far_r, 1), shifted(far_l, -1)
    near_l = shifted(near_l, -1)
    near_r = shifted(near_r, 1)
    to_right, to_left = run(
        merge_kernel, (shape_of(part, BF16), shape_of(part, BF16)), keep_r, keep_l, from_l, from_r
    )
    last_l, last_r = shifted(to_right, 1), shifted(to_left, -1)
    parts = run(ring_sum_kernel, shape_of(whole, BF16), own, near_r, near_l, last_l, last_r)
    out = shape_of((rows, LANES), BF16)
    return run(last_sum_kernel, (out, out), exchanged(parts, "z"))


def solution(mesh):
    split = Mesh(mesh.devices.reshape((4, 2, 8, 4)), ("y", "core", "z", "x"))
    chan = ("z", "x")
    in_specs = (
        P(SEQ, chan),
        P(None, None, chan),
        P(None, None, chan),
        P(None, SEQ, chan),
        P(None, chan),
        P(chan, None),
        P(SEQ, chan),
    )
    out_specs = (P(SEQ, chan), P(SEQ, chan))

    return jax.shard_map(
        on_device, mesh=split, in_specs=in_specs, out_specs=out_specs, check_vma=False
    )
```

```python
import functools
import math

import jax
import jax.numpy as jnp
import numpy as np
from jax import lax
from jax.experimental import pallas as pl
from jax.experimental.pallas import tpu as pltpu
from jax.sharding import Mesh, PartitionSpec as P


F32 = jnp.float32
BF16 = jnp.bfloat16
LANES = 128
BLOCKS = 8
COARSE = 2 * BLOCKS
KEPT = COARSE // 2 + 1
SEQ = ("y", "core")
NEAR_FIRST = (0, 1, 3, 2)


def fine_table():
    ids = np.arange(LANES)
    angle = 2.0 * np.pi / LANES * (ids[:, None] * ids[None, :] % LANES)
    table = np.stack([np.cos(angle), np.sin(angle)]).astype(np.float32)
    high = table.astype(jnp.bfloat16)
    low = (table - high.astype(np.float32)).astype(jnp.bfloat16)
    return np.stack([high, low])


def fine_matrices(table_ref):
    found = []
    for part in range(2):
        cosine, sine = table_ref[part, 0], table_ref[part, 1]
        upper = jnp.concatenate([cosine, -sine], axis=1)
        found.append(jnp.concatenate([upper, jnp.concatenate([sine, cosine], axis=1)], axis=0))
    return found


def twiddle_table():
    angle = (
        2.0 * np.pi / (COARSE * LANES) * (np.arange(KEPT)[:, None] * np.arange(LANES)[None, :])
    )
    return np.stack([np.cos(angle), np.sin(angle)]).astype(np.float32)


def coarse(index):
    index = index % COARSE
    cosine = math.cos(2.0 * math.pi * index / COARSE)
    sine = math.sin(2.0 * math.pi * index / COARSE)
    return cosine, sine


def add_term(total, value, factor):
    if abs(factor) < 1e-9:
        return total
    if abs(abs(factor) - 1.0) < 1e-9:
        if total is None:
            return value if factor > 0 else -value
        return total + value if factor > 0 else total - value
    return value * factor if total is None else total + value * factor


def precise_dot(value, matrices):
    high = value.astype(BF16)
    low = (value - high.astype(F32)).astype(BF16)
    dot = functools.partial(jnp.dot, preferred_element_type=F32)
    return (dot(low, matrices[0]) + dot(high, matrices[1])) + dot(high, matrices[0])


def spectrum(signal, matrices, twiddle_ref):
    parts = []
    for freq in range(KEPT):
        real = imag = None
        for block in range(BLOCKS):
            cosine, sine = coarse(block * freq)
            real = add_term(real, signal[block], cosine)
            imag = add_term(imag, signal[block], -sine)
        cos_t = twiddle_ref[0, freq : freq + 1, :]
        sin_t = twiddle_ref[1, freq : freq + 1, :]
        if imag is None:
            turned = (real * cos_t, -real * sin_t)
        else:
            turned = (real * cos_t + imag * sin_t, imag * cos_t - real * sin_t)
        parts.append(jnp.concatenate(turned, axis=1))
    return precise_dot(jnp.concatenate(parts, axis=0), matrices)


def restore(turned_spec, matrices, twiddle_ref):
    rows = turned_spec.shape[0] // KEPT
    back = precise_dot(turned_spec, matrices)
    real, imag = [], []
    for freq in range(KEPT):
        piece = back[freq * rows : (freq + 1) * rows]
        re, minus_im = piece[:, :LANES], piece[:, LANES:]
        cos_t = twiddle_ref[0, freq : freq + 1, :]
        sin_t = twiddle_ref[1, freq : freq + 1, :]
        real.append(re * cos_t + minus_im * sin_t)
        imag.append(re * sin_t - minus_im * cos_t)
    out = []
    for block in range(BLOCKS):
        total = None
        for freq in range(1, KEPT - 1):
            cosine, sine = coarse(block * freq)
            total = add_term(total, real[freq], cosine)
            total = add_term(total, imag[freq], -sine)
        total = 2.0 * total + real[0]
        out.append(add_term(total, real[KEPT - 1], 1.0 if block % 2 == 0 else -1.0))
    return out


def turned_product(left, right, conjugate):
    left_re, left_im = left[:, :LANES], left[:, LANES:]
    right_re, right_im = right[:, :LANES], right[:, LANES:]
    straight, crossed = left_re * right_re, left_im * right_im
    if conjugate:
        real, minus_imag = straight + crossed, left_re * right_im - left_im * right_re
    else:
        real, minus_imag = straight - crossed, -(left_re * right_im + left_im * right_re)
    return jnp.concatenate([real, minus_imag], axis=1)


def lagged(blocks, steps):
    lane = lax.broadcasted_iota(jnp.int32, blocks[0].shape, 1)
    turned = [pltpu.roll(block, steps, 1) for block in blocks]
    before = [jnp.zeros_like(blocks[0])] + turned[:-1]
    return [jnp.where(lane >= steps, own, prior) for own, prior in zip(turned, before)]


def leading(blocks, steps):
    lane = lax.broadcasted_iota(jnp.int32, blocks[0].shape, 1)
    turned = [pltpu.roll(block, LANES - steps, 1) for block in blocks]
    after = turned[1:] + [jnp.zeros_like(blocks[0])]
    return [jnp.where(lane < LANES - steps, own, later) for own, later in zip(turned, after)]


def short_sum(blocks, coef_ref, which, shift):
    total = [coef_ref[which] * block for block in blocks]
    for tap in (1, 2):
        factor = coef_ref[3 * tap + which]
        total = [have + factor * block for have, block in zip(total, shift(blocks, tap))]
    return total


def operator_kernel(
    place_ref,
    table_hbm,
    twiddle_hbm,
    taps_hbm,
    gains_hbm,
    given_ref,
    filter_ref,
    out_ref,
    table_ref,
    twiddle_ref,
    taps_ref,
    gains_ref,
    rows_ref,
    turned_ref,
    coef_ref,
    sems,
):
    count = given_ref.shape[1] // 4
    tables_in = [
        *started([table_hbm], [table_ref], sems.at[0]),
        *started([twiddle_hbm], [twiddle_ref], sems.at[1]),
    ]
    coef_in = [
        *started([taps_hbm], [taps_ref], sems.at[2]),
        *started([gains_hbm], [gains_ref], sems.at[3]),
    ]
    for copy in coef_in:
        copy.wait()
    rows_ref[...] = jnp.zeros_like(rows_ref)
    for tap in range(3):
        for which in range(3):
            rows_ref[3 * tap + which] = taps_ref[tap, which]
    for order in range(2):
        rows_ref[9 + order] = gains_ref[order]
    turned_ref[...] = rows_ref[...].T
    own_start = pl.multiple_of(place_ref[0] * count, count)
    columns = turned_ref[pl.ds(own_start, count), :]
    for at in range(coef_ref.shape[0]):
        coef_ref[at] = jnp.broadcast_to(columns[:, at : at + 1], coef_ref.shape[1:])

    def rows_of(slot, ref=given_ref):
        return [ref[block, slot * count : (slot + 1) * count] for block in range(BLOCKS)]

    def store(slot, blocks):
        for block, value in enumerate(blocks):
            out_ref[block, slot * count : (slot + 1) * count] = value.astype(BF16)

    def scaled(gain, blocks):
        return [coef_ref[gain] * value for value in blocks]

    def product(left, right):
        return [one * two for one, two in zip(left, right)]

    def plus(left, right):
        return [one + two for one, two in zip(left, right)]

    def filtered(blocks, order, conjugate):
        spec = turned_product(
            spectrum(blocks, matrices, twiddle_ref), filter_spec[order], conjugate
        )
        return plus(restore(spec, matrices, twiddle_ref), scaled(9 + order, blocks))

    values = short_sum(rows_of(0), coef_ref, 0, lagged)
    gate_one = short_sum(rows_of(1), coef_ref, 1, lagged)
    gate_two = short_sum(rows_of(2), coef_ref, 2, lagged)
    for copy in tables_in:
        copy.wait()
    matrices = fine_matrices(table_ref)
    filter_spec = [
        spectrum(rows_of(order, filter_ref), matrices, twiddle_ref) * (1.0 / (COARSE * LANES))
        for order in range(2)
    ]
    conv_one = filtered(values, 0, False)
    conv_two = filtered(product(gate_one, conv_one), 1, False)
    store(0, product(gate_two, conv_two))
    grad_two = rows_of(3)
    store(3, short_sum(product(grad_two, conv_two), coef_ref, 2, leading))
    grad_first = filtered(product(grad_two, gate_two), 1, True)
    store(2, short_sum(product(grad_first, conv_one), coef_ref, 1, leading))
    grad_values = filtered(product(grad_first, gate_one), 0, True)
    store(1, short_sum(grad_values, coef_ref, 0, leading))


def started(source_refs, targets, sems):
    found = []
    for at, (source, target) in enumerate(zip(source_refs, targets)):
        copy = pltpu.make_async_copy(source, target, sems.at[at])
        copy.start()
        found.append(copy)
    return found


def copies_kernel(tokens_hbm, cotangent_hbm, out_ref, held, sems):
    begun = started([tokens_hbm, cotangent_hbm], [held.at[0], held.at[1]], sems)
    for copy in begun:
        copy.wait()
    for at in range(out_ref.shape[0]):
        out_ref[at] = held[...]


def halves_kernel(left_hbm, right_hbm, low_ref, high_ref, sems):
    half = low_ref.shape[0]
    sources = [left_hbm.at[pl.ds(0, half)], right_hbm.at[pl.ds(half, half)]]
    for copy in started(sources, [low_ref, high_ref], sems):
        copy.wait()


def turned_filters_kernel(filter_ref, out_ref):
    count = out_ref.shape[1] // 2
    for order in range(2):
        turned = filter_ref[order].T
        for block in range(BLOCKS):
            out_ref[block, order * count : (order + 1) * count] = turned[
                block * count : (block + 1) * count
            ]


def weights_kernel(place_ref, in_hbm, in_ref, sems):
    parts, _, ring, _, chans = in_hbm.shape
    begun = []
    for slot, apart in enumerate(NEAR_FIRST):
        source = lax.rem(place_ref[0] + apart, ring)
        for part in range(parts):
            copy = pltpu.make_async_copy(
                in_hbm.at[part, :, source],
                in_ref.at[:, slot, :, pl.ds(part * chans, chans)],
                sems.at[slot, part],
            )
            copy.start()
            begun.append(copy)
    for copy in begun:
        copy.wait()


def ring_columns(place_ref, weight_ref, ring, feats, z):
    found = []
    for apart in NEAR_FIRST:
        block = z * ring + lax.rem(place_ref[0] + apart, ring)
        found.append(weight_ref[:, pl.ds(pl.multiple_of(block * feats, feats), feats)])
    return jnp.concatenate(found, axis=1)


def near_kernel(
    place_ref,
    out_hbm,
    weight_ref,
    own,
    left,
    right,
    rows_ref,
    grads_ref,
    far_weight_ref,
    out_weight_ref,
    sems,
):
    (weight_copy,) = started([out_hbm], [out_weight_ref], sems)
    n_z, _, tokens, feats = own.shape
    ring, columns = weight_ref.shape[1], weight_ref.shape[3]

    def near(which, z):
        return jnp.concatenate([ref[z, which] for ref in (own, right, left)], axis=1)

    total = jnp.zeros((tokens, columns), F32)
    for z in range(n_z):
        total = total + jnp.dot(
            near(0, z),
            weight_ref[z, : ring - 1].reshape((-1, columns)),
            preferred_element_type=F32,
        )
    rows_ref[...] = total
    weight_copy.wait()
    total = jnp.zeros((out_weight_ref.shape[0], tokens), F32)
    for z in range(n_z):
        turned = ring_columns(place_ref, out_weight_ref, ring, feats, z)
        far_weight_ref[z] = turned[:, (ring - 1) * feats :]
        total = total + lax.dot_general(
            turned[:, : (ring - 1) * feats],
            near(1, z),
            (((1,), (1,)), ((), ())),
            preferred_element_type=F32,
        )
    grads_ref[...] = total


def far_kernel(weight_ref, far_weight_ref, rows_ref, grads_ref, low, high, out_ref):
    n_z, last = weight_ref.shape[0], weight_ref.shape[1] - 1
    half = low.shape[0]
    chans = far_weight_ref.shape[1]
    count = chans // BLOCKS
    rows, grads = rows_ref[...], grads_ref[...]
    for z in range(n_z):
        far = low.at[z] if z < half else high.at[z - half]
        rows = rows + jnp.dot(far[0], weight_ref[z, last], preferred_element_type=F32)
        grads = grads + lax.dot_general(
            far_weight_ref[z], far[1], (((1,), (1,)), ((), ())), preferred_element_type=F32
        )

    def store(slot, turned):
        for block in range(BLOCKS):
            out_ref[block, slot * count : (slot + 1) * count] = turned[
                block * count : (block + 1) * count
            ]

    for which in range(3):
        store(which, rows[:, which * chans : (which + 1) * chans].T)
    store(3, grads)


def far_partial_kernel(
    place_ref,
    out_hbm,
    in_weight_ref,
    channels_ref,
    far_r_ref,
    far_l_ref,
    out_weight_ref,
    sems,
):
    half, _, feats, tokens = far_r_ref.shape
    n_z = 2 * half
    ring = in_weight_ref.shape[1]
    (weight_copy,) = started([out_hbm], [out_weight_ref], sems)
    count = channels_ref.shape[1] // 4
    second, *grads = [
        channels_ref[:, slot * count : (slot + 1) * count].reshape((BLOCKS * count, tokens))
        for slot in range(4)
    ]
    second = second.astype(F32).T.astype(BF16)
    grads = jnp.concatenate(grads, axis=0)
    wide = out_weight_ref.shape[1] // n_z

    def mixed(z):
        columns_of = ring_columns(place_ref, out_weight_ref, ring, feats, z)
        return jnp.dot(second, columns_of[:, wide - feats :], preferred_element_type=F32)

    def token_grad(z):
        return jnp.dot(in_weight_ref[z, ring - 1], grads, preferred_element_type=F32)

    for output, product in ((1, token_grad), (0, mixed)):
        if output == 0:
            weight_copy.wait()
        for z in range(n_z):
            far_ref = far_r_ref.at[z] if z < half else far_l_ref.at[z - half]
            far_ref[output] = product(z).astype(BF16)


def partial_kernel(
    place_ref,
    out_hbm,
    in_weight_ref,
    channels_ref,
    own_ref,
    near_r_ref,
    near_l_ref,
    keep_r_ref,
    keep_l_ref,
    out_weight_ref,
    sems,
):
    n_z, _, feats, tokens = own_ref.shape
    half = n_z // 2
    ring = in_weight_ref.shape[1]
    (weight_copy,) = started([out_hbm], [out_weight_ref], sems)
    count = channels_ref.shape[1] // 4
    second, *grads = [
        channels_ref[:, slot * count : (slot + 1) * count].reshape((BLOCKS * count, tokens))
        for slot in range(4)
    ]
    second = second.astype(F32).T.astype(BF16)
    grads = jnp.concatenate(grads, axis=0)
    wide = out_weight_ref.shape[1] // n_z
    columns = in_weight_ref.shape[3]

    def mixed(z):
        product = jnp.dot(
            second,
            ring_columns(place_ref, out_weight_ref, ring, feats, z),
            preferred_element_type=F32,
        )
        return [product[:, at : at + feats].astype(BF16) for at in range(0, wide, feats)]

    def token_grad(z):
        product = jnp.dot(
            in_weight_ref[z].reshape((-1, columns)), grads, preferred_element_type=F32
        )
        return [product[at : at + feats].astype(BF16) for at in range(0, wide, feats)]

    for output, pieces in ((1, token_grad), (0, mixed)):
        if output == 0:
            weight_copy.wait()
        for z in range(n_z):
            own, ahead, behind, _ = pieces(z)
            own_ref[z, output] = own
            if z < half:
                keep_r_ref[z, output] = ahead
                near_l_ref[z, output] = behind
            else:
                near_r_ref[z - half, output] = ahead
                keep_l_ref[z - half, output] = behind


def merge_kernel(keep_r_ref, keep_l_ref, from_l_ref, from_r_ref, right_ref, left_ref):
    right_ref[...] = (keep_r_ref[...].astype(F32) + from_l_ref[...].astype(F32)).astype(BF16)
    left_ref[...] = (keep_l_ref[...].astype(F32) + from_r_ref[...].astype(F32)).astype(BF16)


def ring_sum_kernel(own_ref, near_l_ref, near_r_ref, last_l_ref, last_r_ref, out_ref):
    half = last_l_ref.shape[0]
    own_low, own_high = own_ref[:half].astype(F32), own_ref[half:].astype(F32)
    out_ref[:half] = (
        own_low + last_l_ref[...].astype(F32) + near_r_ref[...].astype(F32)
    ).astype(BF16)
    out_ref[half:] = (
        own_high + near_l_ref[...].astype(F32) + last_r_ref[...].astype(F32)
    ).astype(BF16)


def last_sum_kernel(parts_ref, mixed_ref, token_grad_ref):
    totals = []
    for output in range(2):
        total = parts_ref[0, output].astype(F32)
        for part in range(1, parts_ref.shape[0]):
            total = total + parts_ref[part, output].astype(F32)
        totals.append(total)
    mixed_ref[...] = totals[0].astype(BF16)
    token_grad_ref[...] = totals[1].T.astype(BF16)


def run(kernel, out_shape, *args, flops=0, place=None, far=(), scratch=()):
    single = not isinstance(out_shape, (list, tuple))
    outs = (out_shape,) if single else out_shape
    in_vmem = pl.BlockSpec(memory_space=pltpu.VMEM)
    places = () if place is None else (place,)
    specs = [
        *[pl.BlockSpec(memory_space=pltpu.SMEM)] * len(places),
        *[pl.BlockSpec(memory_space=pltpu.HBM)] * len(far),
        *[in_vmem] * len(args),
    ]
    held = (pltpu.with_memory_space_constraint(array, pltpu.HBM) for array in far)
    args = (*places, *held, *args)
    moved = sum(int(np.prod(a.shape)) * a.dtype.itemsize for a in (*args, *outs))
    return pl.pallas_call(
        kernel,
        out_shape=out_shape,
        in_specs=specs,
        out_specs=in_vmem if single else [in_vmem] * len(outs),
        scratch_shapes=scratch,
        compiler_params=pltpu.CompilerParams(vmem_limit_bytes=24 << 20),
        cost_estimate=pl.CostEstimate(flops=flops, bytes_accessed=moved, transcendentals=0),
    )(*args)


def shape_of(shape, dtype):
    return jax.ShapeDtypeStruct(shape, dtype)


def exchanged(value, axis):
    return lax.all_to_all(value, axis, 0, 0, tiled=True)


def shifted(value, steps):
    ring = lax.axis_size("x")
    return lax.ppermute(value, "x", [(at, (at + steps) % ring) for at in range(ring)])


def after(value, *others):
    return lax.optimization_barrier((value, *others))[0]


def on_device(tokens, in_weight, short_kernel, filters, skip_gain, out_weight, cotangent):
    width, _, chans = in_weight.shape
    rows = tokens.shape[0]
    n_z, ring = lax.axis_size("z"), lax.axis_size("x")
    half = n_z // 2
    count = chans // BLOCKS
    seq_place = lax.axis_index(SEQ).reshape((1,)).astype(jnp.int32)
    place = lax.axis_index("x").reshape((1,)).astype(jnp.int32)
    table = jnp.asarray(fine_table())
    twiddles = jnp.asarray(twiddle_table())
    split_in = in_weight.transpose((1, 0, 2)).reshape((3, n_z, ring, LANES, chans))

    sent = run(
        copies_kernel,
        shape_of((n_z, 2, rows, LANES), BF16),
        far=(tokens, cotangent),
        scratch=[pltpu.VMEM((2, rows, LANES), BF16), pltpu.SemaphoreType.DMA((2,))],
    )
    both = exchanged(sent, "z")
    left, right = shifted(both, 1), shifted(both, -1)
    some = shape_of((half, 2, rows, LANES), BF16)
    low, high = run(
        halves_kernel, (some, some), far=(left, right), scratch=[pltpu.SemaphoreType.DMA((2,))]
    )
    low, high = shifted(low, 1), shifted(high, -1)

    turned_filters = run(
        turned_filters_kernel, shape_of((BLOCKS, 2 * count, rows), F32), after(filters, both)
    )
    turned_filters = exchanged(turned_filters, SEQ)
    in_turned = run(
        weights_kernel,
        shape_of((n_z, ring, LANES, 3 * chans), BF16),
        far=(after(split_in, both),),
        place=place,
        scratch=[pltpu.SemaphoreType.DMA((ring, 3))],
    )
    out_scratch = [pltpu.VMEM(out_weight.shape, BF16), pltpu.SemaphoreType.DMA((1,))]
    *near, far_weight = run(
        near_kernel,
        (
            shape_of((rows, 3 * chans), F32),
            shape_of((chans, rows), F32),
            shape_of((n_z, chans, LANES), BF16),
        ),
        in_turned,
        both,
        left,
        right,
        flops=2 * rows * width * 3 * chans,
        place=place,
        far=(out_weight,),
        scratch=out_scratch,
    )
    given = run(
        far_kernel,
        shape_of((BLOCKS, 4 * count, rows), F32),
        in_turned,
        far_weight,
        *near,
        low,
        high,
        flops=2 * rows * width * chans,
    )
    channels = run(
        operator_kernel,
        shape_of((BLOCKS, 4 * count, LANES), BF16),
        exchanged(given, SEQ),
        turned_filters,
        place=seq_place,
        far=(table, twiddles, short_kernel, skip_gain),
        scratch=[
            pltpu.VMEM(table.shape, BF16),
            pltpu.VMEM(twiddles.shape, F32),
            pltpu.VMEM(short_kernel.shape, F32),
            pltpu.VMEM(skip_gain.shape, F32),
            pltpu.VMEM((16, chans), F32),
            pltpu.VMEM((chans, 16), F32),
            pltpu.VMEM((11, count, LANES), F32),
            pltpu.SemaphoreType.DMA((4, 1)),
        ],
    )
    whole, part = (n_z, 2, LANES, rows), (half, 2, LANES, rows)
    channels = exchanged(channels, SEQ)
    far_r, far_l = run(
        far_partial_kernel,
        (shape_of(part, BF16),) * 2,
        in_turned,
        channels,
        flops=rows * width * 2 * chans,
        place=place,
        far=(out_weight,),
        scratch=out_scratch,
    )
    from_l, from_r = shifted(far_r, 1), shifted(far_l, -1)
    own, near_r, near_l, keep_r, keep_l = run(
        partial_kernel,
        tuple(shape_of(shape, BF16) for shape in (whole, *[part] * 4)),
        in_turned,
        channels,
        flops=rows * width * 6 * chans,
        place=place,
        far=(out_weight,),
        scratch=out_scratch,
    )
    near_l = shifted(near_l, -1)
    near_r = shifted(near_r, 1)
    to_right, to_left = run(
        merge_kernel, (shape_of(part, BF16), shape_of(part, BF16)), keep_r, keep_l, from_l, from_r
    )
    last_l, last_r = shifted(to_right, 1), shifted(to_left, -1)
    parts = run(ring_sum_kernel, shape_of(whole, BF16), own, near_r, near_l, last_l, last_r)
    out = shape_of((rows, LANES), BF16)
    return run(last_sum_kernel, (out, out), exchanged(parts, "z"))


def solution(mesh):
    split = Mesh(mesh.devices.reshape((4, 2, 8, 4)), ("y", "core", "z", "x"))
    chan = ("z", "x")
    in_specs = (
        P(SEQ, chan),
        P(None, None, chan),
        P(None, None, chan),
        P(None, SEQ, chan),
        P(None, chan),
        P(chan, None),
        P(SEQ, chan),
    )
    out_specs = (P(SEQ, chan), P(SEQ, chan))

    return jax.shard_map(
        on_device, mesh=split, in_specs=in_specs, out_specs=out_specs, check_vma=False
    )
```
